256 devices in a mesh: seq: 64 (over z, y, core), head: 4 (over x).
Axes of the slice: x: 4, y: 4, z: 8, core: 2. Of those that a mesh axis runs over, the one named last changes fastest.
Arguments:
- query_in: bfloat16 [16384, 4096], P('seq', 'head'), may hold values from -6 to 6
- key_in: bfloat16 [16384, 4096], P('seq', 'head'), may hold values from -6 to 6
- value_in: bfloat16 [16384, 4096], P('seq', 'head')
- out_grad: bfloat16 [16384, 4096], P('seq', 'head'), may hold values from -6 to 6
- norm_gain: float32 [4096], P('head'), may hold values from 0.5 to 1.5
- doc_ids: int32 [16384], P('seq'), may hold values from 0 to 35, as said below
- start_group: int32 [64], replicated, may hold values from 0 to 62, as said below
Outputs:
- normed: bfloat16 [16384, 4096], P('seq', 'head')
- grad_query: bfloat16 [16384, 4096], P('seq', 'head')
- grad_key: bfloat16 [16384, 4096], P('seq', 'head')
- grad_value: bfloat16 [16384, 4096], P('seq', 'head')
The draws below stay inside these ranges and needn't reach their ends.
Inputs may be any that keep to these rules, and one draw needn't show every extreme that they name: `doc_ids`: 0 at the first token, never falling, one more at each document start. `start_group`: entry c is the block in which the document holding block c's first token begins; it agrees with doc_ids.
All inputs are finite; a program needn't handle non-finite values.
Results may differ from the reference program's by a relative error of at most 0.0058.
Values may be sent and summed in bfloat16 or wider, within the bound.
A program may use at most 128 MiB of HBM per device.

```python
import math
from functools import partial
import jax
import jax.numpy as jnp
from jax import lax

H = 32
HD = 128
TOK_DEV = 256
GROUPS = 64
TOKENS = 16384


def doc_layout(key):
    base = jax.random.fold_in(key, 7)
    places_all = jnp.arange(TOKENS, dtype=jnp.int32)
    priority = jax.random.permutation(jax.random.fold_in(base, 1), TOKENS).astype(jnp.int32)
    other_block = jax.random.randint(jax.random.fold_in(base, 2), (1,), 2, max(GROUPS - 2, 3))
    aligned = jnp.concatenate([jnp.full((1,), GROUPS - 2, jnp.int32), other_block.astype(jnp.int32)]) * TOK_DEV
    boost = jnp.zeros((TOKENS,), jnp.int32).at[aligned].set(TOKENS)
    forbidden = (places_all == 0) | (places_all == TOK_DEV) | (places_all >= (GROUPS - 1) * TOK_DEV)
    priority = jnp.where(forbidden, -1, priority + boost)
    chosen = lax.top_k(priority, GROUPS // 2 + 3)[1]
    marks = jnp.zeros((TOKENS,), jnp.int32).at[chosen].set(1)
    doc_ids = jnp.cumsum(marks).astype(jnp.int32)
    places = jnp.where(marks > 0, places_all, 0)
    begins = lax.cummax(places, axis=0)
    start_group = (begins[::TOK_DEV] // TOK_DEV).astype(jnp.int32)
    return (doc_ids, start_group)


def draw_doc_ids(key, part):
    return doc_layout(key)[0]


def draw_start_group(key, part):
    return doc_layout(key)[1]


def draw_value_in(key, part):
    width = H * HD
    columns = jnp.arange(width, dtype=jnp.float32) / (width - 1)
    noise = jax.random.normal(jax.random.fold_in(key, 1), (TOKENS, width), jnp.float32)
    ramp = 3.0 ** (0.5 * columns)
    col_scale = jnp.exp(jax.random.uniform(jax.random.fold_in(key, 2), (width,), jnp.float32, 0.0, math.log(10.0)))
    row_scale = jnp.exp(jax.random.uniform(jax.random.fold_in(key, 3), (TOKENS, 1), jnp.float32, 0.0, math.log(10.0)))
    return (noise * col_scale * row_scale * ramp * 0.25).astype(jnp.bfloat16)


def steps_of(own_key, shape, cuts, low, top_value):
    def one(position, shards_of):
        draws = jax.random.uniform(jax.random.fold_in(jax.random.fold_in(own_key, 6), position), (shards_of,), jnp.float32, low / len(cuts), top_value / len(cuts))
        return jnp.repeat(jnp.exp(draws), shape[position] // shards_of).reshape((-1,) + (1,) * (len(shape) - position - 1))

    gain = one(*cuts[0])
    for cut in cuts[1:]:
        gain = gain * one(*cut)
    return gain


def bell_draw(rng, shape, deviation, limit, cuts=(), held_as=jnp.bfloat16):
    values = deviation * jax.random.normal(rng, shape, jnp.float32)
    if cuts:
        values = values * steps_of(rng, shape, cuts, -0.22, 0.18)
    return jnp.clip(values, -limit, limit).astype(held_as)


def setup_inputs(seed: int = 0) -> dict:
    streams_of = jax.random.split(jax.random.key(seed), 8)
    return {
        "query_in": bell_draw(streams_of[0], (TOKENS, H * HD), 1.0, 6.0, ((0, 64), (1, 4))),
        "key_in": bell_draw(streams_of[1], (TOKENS, H * HD), 1.0, 6.0, ((0, 64), (1, 4))),
        "value_in": draw_value_in(jax.random.fold_in(streams_of[7], 71), 0),
        "out_grad": bell_draw(streams_of[3], (TOKENS, H * HD), 1.0, 6.0, ((0, 64), (1, 4))),
        "norm_gain": jnp.clip(1.0 + 0.1 * jax.random.normal(streams_of[4], (H * HD,), jnp.float32), 0.5, 1.5),
        "doc_ids": draw_doc_ids(jax.random.fold_in(streams_of[7], 71), 0),
        "start_group": draw_start_group(jax.random.fold_in(streams_of[7], 71), 0),
    }


epsilon = 1e-06
contract = partial(jnp.einsum, precision=lax.Precision.HIGHEST)

def reference(query_in, key_in, value_in, out_grad, norm_gain, doc_ids, start_group):
    width = H * HD

    def blocked(array):
        return array.reshape(GROUPS, TOK_DEV, H, HD)
    query_b = blocked(query_in)
    key_b = blocked(key_in)
    value_b = blocked(value_in)
    grad_b = blocked(out_grad)
    ids_b = doc_ids.reshape(GROUPS, TOK_DEV)
    first_doc = (ids_b == ids_b[:, :1]).astype(jnp.float32)
    last_doc = (ids_b == ids_b[:, -1:]).astype(jnp.float32)
    group_ids = jnp.arange(GROUPS, dtype=jnp.int32)
    causal = jnp.arange(TOK_DEV)[:, None] >= jnp.arange(TOK_DEV)[None, :]
    gain_heads = norm_gain.reshape(H, HD).astype(jnp.float32)

    def tail_of(pieces):
        key_c, value_c, last_c = pieces
        return contract('tha,thb->hab', key_c.astype(jnp.float32) * last_c[:, None, None], value_c.astype(jnp.float32))
    tails = lax.map(tail_of, (key_b, value_b, last_doc))
    forward_mask = ((start_group[:, None] <= group_ids[None, :]) & (group_ids[None, :] < group_ids[:, None])).astype(jnp.float32)
    carries = contract('cj,jhab->chab', forward_mask, tails).astype(jnp.bfloat16)

    def attention_weights(query_f, key_f, ids_c):
        same_doc = causal & (ids_c[:, None] == ids_c[None, :])
        scores = contract('tha,uha->htu', query_f, key_f)
        return (jnp.where(same_doc[None], scores, 0.0).astype(jnp.bfloat16), same_doc)

    def forward_block(pieces):
        query_c, key_c, value_c, grad_c, ids_c, first_c, carry_c = pieces
        query_f = query_c.astype(jnp.float32)
        key_f = key_c.astype(jnp.float32)
        value_f = value_c.astype(jnp.float32)
        grad_f = grad_c.astype(jnp.float32)
        weights, same_doc = attention_weights(query_f, key_f, ids_c)
        attended = contract('htu,uhb->thb', weights.astype(jnp.float32), value_f)
        attended = attended + first_c[:, None, None] * contract('tha,hab->thb', query_f, carry_c.astype(jnp.float32))
        square_total = lax.optimization_barrier(jnp.sum(attended * attended, axis=(1, 2)))
        inverse_rms = lax.rsqrt(square_total / width + epsilon)
        normed = (attended * inverse_rms[:, None, None] * gain_heads).astype(jnp.bfloat16)
        cross_total = lax.optimization_barrier(jnp.sum(gain_heads * grad_f * attended, axis=(1, 2)))
        grad_attended = (inverse_rms[:, None, None] * gain_heads * grad_f - (inverse_rms ** 3 * cross_total / width)[:, None, None] * attended).astype(jnp.bfloat16)
        head_state = contract('tha,thb->hab', query_f * first_c[:, None, None], grad_attended.astype(jnp.float32))
        return (normed, grad_attended, head_state)
    normed, grad_att, heads = lax.map(forward_block, (query_b, key_b, value_b, grad_b, ids_b, first_doc, carries))
    backward_mask = ((start_group[None, :] <= group_ids[:, None]) & (group_ids[:, None] < group_ids[None, :])).astype(jnp.float32)
    dstates = contract('cj,jhab->chab', backward_mask, heads).astype(jnp.bfloat16)

    def backward_block(pieces):
        query_c, key_c, value_c, grad_c, ids_c, first_c, last_c, carry_c, dstate_c = pieces
        query_f = query_c.astype(jnp.float32)
        key_f = key_c.astype(jnp.float32)
        value_f = value_c.astype(jnp.float32)
        grad_f = grad_c.astype(jnp.float32)
        carry_f = carry_c.astype(jnp.float32)
        dstate_f = dstate_c.astype(jnp.float32)
        weights, same_doc = attention_weights(query_f, key_f, ids_c)
        grad_scores = jnp.where(same_doc[None], contract('tha,uha->htu', grad_f, value_f), 0.0).astype(jnp.bfloat16).astype(jnp.float32)
        grad_q = contract('htu,uha->tha', grad_scores, key_f) + first_c[:, None, None] * contract('thb,hab->tha', grad_f, carry_f)
        grad_k = contract('htu,tha->uha', grad_scores, query_f) + last_c[:, None, None] * contract('uhb,hab->uha', value_f, dstate_f)
        grad_v = contract('htu,thb->uhb', weights.astype(jnp.float32), grad_f) + last_c[:, None, None] * contract('uha,hab->uhb', key_f, dstate_f)
        return (grad_q.astype(jnp.bfloat16), grad_k.astype(jnp.bfloat16), grad_v.astype(jnp.bfloat16))
    grad_q, grad_k, grad_v = lax.map(backward_block, (query_b, key_b, value_b, grad_att, ids_b, first_doc, last_doc, carries, dstates))
    shape = (TOKENS, width)
    return (normed.reshape(shape), grad_q.reshape(shape), grad_k.reshape(shape), grad_v.reshape(shape))
```

```python
import functools

import jax
import jax.numpy as jnp
from jax import lax
from jax.experimental import pallas as pl
from jax.experimental.pallas import tpu as pltpu
from jax.sharding import PartitionSpec as P

HD = 128
EPSILON = 1e-06
CHUNKS = 2
MESH = pl.DeviceIdType.MESH
f32, bf16 = jnp.float32, jnp.bfloat16


def dot(a, b, contract):
    return lax.dot_general(a, b, (contract, ((), ())), preferred_element_type=f32)


NN = ((1,), (0,))
NT = ((1,), (1,))
TN = ((0,), (0,))


def kernel(
    planes, heads, spread, width,
    sg_ref, doc_ref, q_ref, k_ref, v_ref, g_ref, gain_ref,
    normed_ref, gq_ref, gk_ref, gv_ref,
    same_ref, first_ref, last_ref, inv_ref, coef_ref,
    weights_ref, att_ref, ga_ref, gk_acc, gv_acc,
    tail_out, tail_in, pre_ref, agg_out, agg_in, carry_out, carry_in,
    head_out, head_in, suf_ref, bagg_out, bagg_in, back_out, back_in,
    sums_out, sums_in,
    plane_send, plane_recv, z_send, z_recv, x_send, x_recv,
):
    seq, col = lax.axis_index("seq"), lax.axis_index("head")
    z, p = lax.div(seq, heads), lax.rem(seq, heads)
    tokens = q_ref.shape[0]
    rows = HD // CHUNKS
    base = z * heads

    def plane_peer(d):
        return lax.rem(p + d, heads)

    barrier = pltpu.get_barrier_semaphore()
    for d in range(1, heads):
        pl.semaphore_signal(barrier, inc=1, device_id=(base + plane_peer(d), col), device_id_type=MESH)
    for d in range(1, planes):
        pl.semaphore_signal(
            barrier, inc=1, device_id=(lax.rem(z + d, planes) * heads + p, col), device_id_type=MESH
        )
    for d in range(1, spread):
        pl.semaphore_signal(barrier, inc=1, device_id=(seq, lax.rem(col + d, spread)), device_id_type=MESH)

    def lanes(h):
        return pl.ds(pl.multiple_of(h * HD, HD), HD)

    def chunk(r):
        return pl.ds(r * rows, rows)

    def start_of(block):
        return sg_ref[block]

    def flag(condition):
        return jnp.where(condition, 1.0, 0.0).astype(f32)

    def plane_copy(phase, src, dst, at_src, at_dst, r, peer):
        return pltpu.make_async_remote_copy(
            src_ref=src.at[at_src, chunk(r)],
            dst_ref=dst.at[at_dst, chunk(r)],
            send_sem=plane_send.at[phase, r, peer],
            recv_sem=plane_recv.at[phase, r, at_dst],
            device_id=(base + peer, col),
            device_id_type=MESH,
        )

    def plane_start(phase, src, dst, r, peer):
        plane_copy(phase, src, dst, peer, p, r, peer).start()

    def plane_wait(phase, src, dst, r, peer):
        copy = plane_copy(phase, src, dst, peer, peer, r, peer)
        copy.wait_send()
        copy.wait_recv()

    def z_copy(phase, src, dst, r, at_dst, peer):
        return pltpu.make_async_remote_copy(
            src_ref=src.at[chunk(r)],
            dst_ref=dst.at[at_dst, chunk(r)],
            send_sem=z_send.at[phase, r, peer],
            recv_sem=z_recv.at[phase, r, at_dst],
            device_id=(peer * heads + p, col),
            device_id_type=MESH,
        )

    doc_row = jnp.broadcast_to(doc_ref[...].astype(f32), (tokens, tokens))
    doc_col = doc_row.T
    causal = lax.broadcasted_iota(jnp.int32, (tokens, tokens), 0) >= lax.broadcasted_iota(
        jnp.int32, (tokens, tokens), 1
    )
    same_ref[...] = jnp.where(causal & (doc_row == doc_col), 1.0, 0.0)
    mine = doc_col[:, :HD]
    first_ref[...] = jnp.where(mine == mine[:1], 1.0, 0.0).astype(bf16)
    last_ref[...] = jnp.where(mine == mine[tokens - 1 :], 1.0, 0.0).astype(bf16)

    for d in range(1, heads + 1):
        h = plane_peer(d)
        tail = dot(k_ref[:, lanes(h)] * last_ref[...], v_ref[:, lanes(h)], TN).astype(bf16)
        if d < heads:
            tail_out[h] = tail
        else:
            tail_in[p] = tail
    pl.semaphore_wait(barrier, heads + planes + spread - 3)
    for r in range(CHUNKS):
        for d in range(1, heads):
            plane_start(0, tail_out, tail_in, r, plane_peer(d))

    def local_forward(h, _):
        scores = dot(q_ref[:, lanes(h)], k_ref[:, lanes(h)], NT)
        weights = jnp.where(same_ref[...] > 0.5, scores, 0.0).astype(bf16)
        weights_ref[h] = weights
        att_ref[:, lanes(h)] = dot(weights, v_ref[:, lanes(h)], NN)
        return _

    lax.fori_loop(0, heads // 2, local_forward, 0)

    groups = planes * heads
    after = jnp.minimum(base + heads, groups - 1)
    for r in range(CHUNKS):
        for d in range(1, heads):
            plane_wait(0, tail_out, tail_in, r, plane_peer(d))
        run = jnp.zeros((rows, HD), f32)
        pre_ref[0, chunk(r)] = run
        for i in range(1, heads + 1):
            begin = start_of(base + i) if i < heads else start_of(after)
            joined = flag(begin < base + i - 1) * run + tail_in[i - 1, chunk(r)].astype(f32)
            run = flag(begin <= base + i - 1) * joined
            if i < heads:
                pre_ref[i, chunk(r)] = run
        agg_out[chunk(r)] = run.astype(bf16)

        def send_up(to, _, r=r):
            z_copy(0, agg_out, agg_in, r, z, to).start()
            return _

        lax.fori_loop(z + 1, planes, send_up, 0)

    lax.fori_loop(heads // 2, heads, local_forward, 0)

    begin_plane = start_of(base)
    for r in range(CHUNKS):

        def join(at, total, r=r):
            z_copy(0, agg_out, agg_in, r, at, at).wait_recv()
            return total + flag(begin_plane <= at * heads + heads - 1) * agg_in[at, chunk(r)].astype(f32)

        total = lax.fori_loop(0, z, join, jnp.zeros((rows, HD), f32))
        for d in range(1, heads + 1):
            i = plane_peer(d)
            carry = (pre_ref[i, chunk(r)] + flag(start_of(base + i) < base) * total).astype(bf16)
            if d < heads:
                carry_out[i, chunk(r)] = carry
                plane_start(1, carry_out, carry_in, r, i)
            else:
                carry_in[p, chunk(r)] = carry

    square = jnp.zeros((tokens, HD), f32)
    cross = jnp.zeros((tokens, HD), f32)
    for d in range(heads):
        h = plane_peer(d)
        if d > 0:
            for r in range(CHUNKS):
                plane_wait(1, carry_out, carry_in, r, h)
        att = att_ref[:, lanes(h)] + dot(q_ref[:, lanes(h)] * first_ref[...], carry_in[h], NN)
        att_ref[:, lanes(h)] = att
        square = square + att * att
        cross = cross + gain_ref[:, lanes(h)] * g_ref[:, lanes(h)].astype(f32) * att
    sums_out[0:1] = jnp.sum(square.T, axis=0, keepdims=True)
    sums_out[1:2] = jnp.sum(cross.T, axis=0, keepdims=True)

    def x_copy(at_dst, peer):
        return pltpu.make_async_remote_copy(
            src_ref=sums_out,
            dst_ref=sums_in.at[at_dst],
            send_sem=x_send.at[peer],
            recv_sem=x_recv.at[at_dst],
            device_id=(seq, peer),
            device_id_type=MESH,
        )

    for d in range(1, spread):
        x_copy(col, lax.rem(col + d, spread)).start()
    sums = sums_out[...]
    for d in range(1, spread):
        peer = lax.rem(col + d, spread)
        copy = x_copy(peer, peer)
        copy.wait_send()
        copy.wait_recv()
        sums = sums + sums_in[peer]
    inverse = lax.rsqrt(sums[0:1] / width + EPSILON)
    coef = inverse * inverse * inverse * sums[1:2] / width
    inv_ref[...] = jnp.broadcast_to(inverse, (HD, tokens)).T
    coef_ref[...] = jnp.broadcast_to(coef, (HD, tokens)).T

    for d in range(1, heads + 1):
        h = plane_peer(d)
        scaled = inv_ref[...] * gain_ref[:, lanes(h)]
        ga = (scaled * g_ref[:, lanes(h)].astype(f32) - coef_ref[...] * att_ref[:, lanes(h)]).astype(bf16)
        ga_ref[:, lanes(h)] = ga
        state = dot(q_ref[:, lanes(h)] * first_ref[...], ga, TN).astype(bf16)
        if d < heads:
            head_out[h] = state
            for r in range(CHUNKS):
                plane_start(2, head_out, head_in, r, h)
        else:
            head_in[p] = state

    def local_backward(h, _):
        ga = ga_ref[:, lanes(h)]
        normed_ref[:, lanes(h)] = (att_ref[:, lanes(h)] * inv_ref[...] * gain_ref[:, lanes(h)]).astype(bf16)
        scores = dot(ga, v_ref[:, lanes(h)], NT)
        scores = jnp.where(same_ref[...] > 0.5, scores, 0.0).astype(bf16)
        part = dot(ga * first_ref[...], carry_in[h], NT)
        gq_ref[:, lanes(h)] = (dot(scores, k_ref[:, lanes(h)], NN) + part).astype(bf16)
        gk_acc[:, lanes(h)] = dot(scores, q_ref[:, lanes(h)], TN)
        gv_acc[:, lanes(h)] = dot(weights_ref[h], ga, TN)
        return _

    lax.fori_loop(0, heads // 2, local_backward, 0)

    for r in range(CHUNKS):
        for d in range(1, heads):
            plane_wait(2, head_out, head_in, r, plane_peer(d))
        total = jnp.zeros((rows, HD), f32)
        for i in range(heads):
            total = total + flag(start_of(base + i) < base) * head_in[i, chunk(r)].astype(f32)
        bagg_out[chunk(r)] = total.astype(bf16)

        def send_down(to, _, r=r):
            z_copy(1, bagg_out, bagg_in, r, z, to).start()
            return _

        lax.fori_loop(0, z, send_down, 0)
        run = jnp.zeros((rows, HD), f32)
        suf_ref[heads - 1, chunk(r)] = run
        for i in range(heads - 2, -1, -1):
            begin = start_of(base + i + 1)
            if i + 2 < heads:
                run = flag(start_of(base + i + 2) <= base + i) * run
            run = flag(begin <= base + i) * (run + head_in[i + 1, chunk(r)].astype(f32))
            suf_ref[i, chunk(r)] = run

    lax.fori_loop(heads // 2, heads, local_backward, 0)

    open_after = jnp.where(z < planes - 1, start_of(after), groups)
    for r in range(CHUNKS):

        def join_back(at, total, r=r):
            z_copy(1, bagg_out, bagg_in, r, at, at).wait_recv()
            return total + flag(start_of(at * heads) <= base + heads - 1) * bagg_in[at, chunk(r)].astype(f32)

        total = lax.fori_loop(z + 1, planes, join_back, jnp.zeros((rows, HD), f32))
        for d in range(1, heads + 1):
            i = plane_peer(d)
            state = (suf_ref[i, chunk(r)] + flag(open_after <= base + i) * total).astype(bf16)
            if d < heads:
                back_out[i, chunk(r)] = state
                plane_start(3, back_out, back_in, r, i)
            else:
                back_in[p, chunk(r)] = state

    for d in range(heads):
        h = plane_peer(d)
        if d > 0:
            for r in range(CHUNKS):
                plane_wait(3, back_out, back_in, r, h)
        last = last_ref[...]
        gk_ref[:, lanes(h)] = (gk_acc[:, lanes(h)] + dot(v_ref[:, lanes(h)] * last, back_in[h], NT)).astype(bf16)
        gv_ref[:, lanes(h)] = (gv_acc[:, lanes(h)] + dot(k_ref[:, lanes(h)] * last, back_in[h], NN)).astype(bf16)

    for r in range(CHUNKS):

        def sent_up(to, _, r=r):
            z_copy(0, agg_out, agg_in, r, to, to).wait_send()
            return _

        def sent_down(to, _, r=r):
            z_copy(1, bagg_out, bagg_in, r, to, to).wait_send()
            return _

        lax.fori_loop(z + 1, planes, sent_up, 0)
        lax.fori_loop(0, z, sent_down, 0)


def solution(mesh):
    groups, spread = mesh.shape["seq"], mesh.shape["head"]

    def local(query_in, key_in, value_in, out_grad, norm_gain, doc_ids, start_group):
        tokens, columns = query_in.shape
        heads = columns // HD
        planes = groups // heads
        vmem = pl.BlockSpec(memory_space=pltpu.VMEM)
        state = pltpu.VMEM((heads, HD, HD), bf16)
        state_f = pltpu.VMEM((heads, HD, HD), f32)
        one = pltpu.VMEM((HD, HD), bf16)
        many = pltpu.VMEM((planes, HD, HD), bf16)
        row = pltpu.VMEM((tokens, HD), f32)
        scan = [state, state, state_f, one, many, state, state]
        return pl.pallas_call(
            functools.partial(kernel, planes, heads, spread, columns * spread),
            out_shape=[jax.ShapeDtypeStruct((tokens, columns), bf16)] * 4,
            in_specs=[pl.BlockSpec(memory_space=pltpu.SMEM)] + [vmem] * 6,
            out_specs=[vmem] * 4,
            scratch_shapes=[
                pltpu.VMEM((tokens, tokens), f32),
                pltpu.VMEM((tokens, HD), bf16),
                pltpu.VMEM((tokens, HD), bf16),
                row,
                row,
                pltpu.VMEM((heads, tokens, tokens), bf16),
                pltpu.VMEM((tokens, columns), f32),
                pltpu.VMEM((tokens, columns), bf16),
                pltpu.VMEM((tokens, columns), f32),
                pltpu.VMEM((tokens, columns), f32),
                *scan,
                *scan,
                pltpu.VMEM((2, tokens), f32),
                pltpu.VMEM((spread, 2, tokens), f32),
                pltpu.SemaphoreType.DMA((4, CHUNKS, heads)),
                pltpu.SemaphoreType.DMA((4, CHUNKS, heads)),
                pltpu.SemaphoreType.DMA((2, CHUNKS, planes)),
                pltpu.SemaphoreType.DMA((2, CHUNKS, planes)),
                pltpu.SemaphoreType.DMA((spread,)),
                pltpu.SemaphoreType.DMA((spread,)),
            ],
            compiler_params=pltpu.CompilerParams(collective_id=0, has_side_effects=True),
            name="attention",
        )(
            start_group,
            doc_ids.reshape(1, tokens),
            query_in,
            key_in,
            value_in,
            out_grad,
            norm_gain.reshape(1, columns),
        )

    wide = P("seq", "head")
    return jax.shard_map(
        local,
        mesh=mesh,
        in_specs=(wide, wide, wide, wide, P("head"), P("seq"), P()),
        out_specs=(wide, wide, wide, wide),
        check_vma=False,
    )
```

```python
import functools

import jax
import jax.numpy as jnp
from jax import lax
from jax.experimental import pallas as pl
from jax.experimental.pallas import tpu as pltpu
from jax.sharding import PartitionSpec as P

HD = 128
EPSILON = 1e-06
CHUNKS = 2
MESH = pl.DeviceIdType.MESH
f32, bf16 = jnp.float32, jnp.bfloat16


def dot(a, b, contract):
    return lax.dot_general(a, b, (contract, ((), ())), preferred_element_type=f32)


NN = ((1,), (0,))
NT = ((1,), (1,))
TN = ((0,), (0,))


def kernel(
    planes, heads, spread, width,
    sg_ref, doc_ref, q_ref, k_ref, v_ref, g_ref, gain_ref,
    normed_ref, gq_ref, gk_ref, gv_ref,
    same_ref, first_ref, last_ref, inv_ref, coef_ref,
    weights_ref, att_ref, ga_ref, gk_acc, gv_acc,
    tail_out, tail_in, pre_ref, agg_out, agg_in, carry_out, carry_in,
    head_out, head_in, suf_ref, bagg_out, bagg_in, back_out, back_in,
    sums_out, sums_in,
    plane_send, plane_recv, z_send, z_recv, x_send, x_recv,
):
    seq, col = lax.axis_index("seq"), lax.axis_index("head")
    z, p = lax.div(seq, heads), lax.rem(seq, heads)
    tokens = q_ref.shape[0]
    rows = HD // CHUNKS
    base = z * heads

    def plane_peer(d):
        return lax.rem(p + d, heads)

    barrier = pltpu.get_barrier_semaphore()
    for d in range(1, heads):
        pl.semaphore_signal(barrier, inc=1, device_id=(base + plane_peer(d), col), device_id_type=MESH)
    for d in range(1, planes):
        pl.semaphore_signal(
            barrier, inc=1, device_id=(lax.rem(z + d, planes) * heads + p, col), device_id_type=MESH
        )
    for d in range(1, spread):
        pl.semaphore_signal(barrier, inc=1, device_id=(seq, lax.rem(col + d, spread)), device_id_type=MESH)

    def lanes(h):
        return pl.ds(pl.multiple_of(h * HD, HD), HD)

    def chunk(r):
        return pl.ds(r * rows, rows)

    def start_of(block):
        return sg_ref[block]

    def flag(condition):
        return jnp.where(condition, 1.0, 0.0).astype(f32)

    def plane_copy(phase, src, dst, at_src, at_dst, r, peer):
        return pltpu.make_async_remote_copy(
            src_ref=src.at[at_src, chunk(r)],
            dst_ref=dst.at[at_dst, chunk(r)],
            send_sem=plane_send.at[phase, r, peer],
            recv_sem=plane_recv.at[phase, r, at_dst],
            device_id=(base + peer, col),
            device_id_type=MESH,
        )

    def plane_start(phase, src, dst, r, peer):
        plane_copy(phase, src, dst, peer, p, r, peer).start()

    def plane_wait(phase, src, dst, r, peer):
        copy = plane_copy(phase, src, dst, peer, peer, r, peer)
        copy.wait_send()
        copy.wait_recv()

    def z_copy(phase, src, dst, r, at_dst, peer):
        return pltpu.make_async_remote_copy(
            src_ref=src.at[chunk(r)],
            dst_ref=dst.at[at_dst, chunk(r)],
            send_sem=z_send.at[phase, r, peer],
            recv_sem=z_recv.at[phase, r, at_dst],
            device_id=(peer * heads + p, col),
            device_id_type=MESH,
        )

    doc_row = jnp.broadcast_to(doc_ref[...].astype(f32), (tokens, tokens))
    doc_col = doc_row.T
    causal = lax.broadcasted_iota(jnp.int32, (tokens, tokens), 0) >= lax.broadcasted_iota(
        jnp.int32, (tokens, tokens), 1
    )
    same_ref[...] = jnp.where(causal & (doc_row == doc_col), 1.0, 0.0)
    mine = doc_col[:, :HD]
    first_ref[...] = jnp.where(mine == mine[:1], 1.0, 0.0).astype(bf16)
    last_ref[...] = jnp.where(mine == mine[tokens - 1 :], 1.0, 0.0).astype(bf16)

    for d in range(1, heads + 1):
        h = plane_peer(d)
        tail = dot(k_ref[:, lanes(h)] * last_ref[...], v_ref[:, lanes(h)], TN).astype(bf16)
        if d < heads:
            tail_out[h] = tail
        else:
            tail_in[p] = tail
    pl.semaphore_wait(barrier, heads + planes + spread - 3)
    for r in range(CHUNKS):
        for d in range(1, heads):
            plane_start(0, tail_out, tail_in, r, plane_peer(d))

    def local_forward(h, _):
        scores = dot(q_ref[:, lanes(h)], k_ref[:, lanes(h)], NT)
        weights = jnp.where(same_ref[...] > 0.5, scores, 0.0).astype(bf16)
        weights_ref[h] = weights
        att_ref[:, lanes(h)] = dot(weights, v_ref[:, lanes(h)], NN)
        return _

    lax.fori_loop(0, heads // 2, local_forward, 0)

    groups = planes * heads
    after = jnp.minimum(base + heads, groups - 1)
    for r in range(CHUNKS):
        for d in range(1, heads):
            plane_wait(0, tail_out, tail_in, r, plane_peer(d))
        run = jnp.zeros((rows, HD), f32)
        pre_ref[0, chunk(r)] = run
        for i in range(1, heads + 1):
            begin = start_of(base + i) if i < heads else start_of(after)
            joined = flag(begin < base + i - 1) * run + tail_in[i - 1, chunk(r)].astype(f32)
            run = flag(begin <= base + i - 1) * joined
            if i < heads:
                pre_ref[i, chunk(r)] = run
        agg_out[chunk(r)] = run.astype(bf16)

        def send_up(to, _, r=r):
            z_copy(0, agg_out, agg_in, r, z, to).start()
            return _

        lax.fori_loop(z + 1, planes, send_up, 0)

    lax.fori_loop(heads // 2, heads, local_forward, 0)

    begin_plane = start_of(base)
    for r in range(CHUNKS):

        def join(at, total, r=r):
            z_copy(0, agg_out, agg_in, r, at, at).wait_recv()
            return total + flag(begin_plane <= at * heads + heads - 1) * agg_in[at, chunk(r)].astype(f32)

        total = lax.fori_loop(0, z, join, jnp.zeros((rows, HD), f32))
        for d in range(1, heads + 1):
            i = plane_peer(d)
            carry = (pre_ref[i, chunk(r)] + flag(start_of(base + i) < base) * total).astype(bf16)
            if d < heads:
                carry_out[i, chunk(r)] = carry
                plane_start(1, carry_out, carry_in, r, i)
            else:
                carry_in[p, chunk(r)] = carry

    square = jnp.zeros((tokens, HD), f32)
    cross = jnp.zeros((tokens, HD), f32)
    for d in range(heads):
        h = plane_peer(d)
        if d > 0:
            for r in range(CHUNKS):
                plane_wait(1, carry_out, carry_in, r, h)
        att = att_ref[:, lanes(h)] + dot(q_ref[:, lanes(h)] * first_ref[...], carry_in[h], NN)
        att_ref[:, lanes(h)] = att
        square = square + att * att
        cross = cross + gain_ref[:, lanes(h)] * g_ref[:, lanes(h)].astype(f32) * att
    sums_out[0:1] = jnp.sum(square.T, axis=0, keepdims=True)
    sums_out[1:2] = jnp.sum(cross.T, axis=0, keepdims=True)

    def x_copy(at_dst, peer):
        return pltpu.make_async_remote_copy(
            src_ref=sums_out,
            dst_ref=sums_in.at[at_dst],
            send_sem=x_send.at[peer],
            recv_sem=x_recv.at[at_dst],
            device_id=(seq, peer),
            device_id_type=MESH,
        )

    for d in range(1, spread):
        x_copy(col, lax.rem(col + d, spread)).start()
    sums = sums_out[...]
    for d in range(1, spread):
        peer = lax.rem(col + d, spread)
        copy = x_copy(peer, peer)
        copy.wait_send()
        copy.wait_recv()
        sums = sums + sums_in[peer]
    inverse = lax.rsqrt(sums[0:1] / width + EPSILON)
    coef = inverse * inverse * inverse * sums[1:2] / width
    inv_ref[...] = jnp.broadcast_to(inverse, (HD, tokens)).T
    coef_ref[...] = jnp.broadcast_to(coef, (HD, tokens)).T

    for d in range(1, heads + 1):
        h = plane_peer(d)
        scaled = inv_ref[...] * gain_ref[:, lanes(h)]
        ga = (scaled * g_ref[:, lanes(h)].astype(f32) - coef_ref[...] * att_ref[:, lanes(h)]).astype(bf16)
        ga_ref[:, lanes(h)] = ga
        state = dot(q_ref[:, lanes(h)] * first_ref[...], ga, TN).astype(bf16)
        if d < heads:
            head_out[h] = state
            for r in range(CHUNKS):
                plane_start(2, head_out, head_in, r, h)
        else:
            head_in[p] = state

    def local_backward(h, _):
        ga = ga_ref[:, lanes(h)]
        normed_ref[:, lanes(h)] = (att_ref[:, lanes(h)] * inv_ref[...] * gain_ref[:, lanes(h)]).astype(bf16)
        scores = dot(ga, v_ref[:, lanes(h)], NT)
        scores = jnp.where(same_ref[...] > 0.5, scores, 0.0).astype(bf16)
        part = dot(ga * first_ref[...], carry_in[h], NT)
        gq_ref[:, lanes(h)] = (dot(scores, k_ref[:, lanes(h)], NN) + part).astype(bf16)
        gk_acc[:, lanes(h)] = dot(scores, q_ref[:, lanes(h)], TN)
        gv_acc[:, lanes(h)] = dot(weights_ref[h], ga, TN)
        return _

    lax.fori_loop(0, heads // 2, local_backward, 0)

    for r in range(CHUNKS):
        for d in range(1, heads):
            plane_wait(2, head_out, head_in, r, plane_peer(d))
        total = jnp.zeros((rows, HD), f32)
        for i in range(heads):
            total = total + flag(start_of(base + i) < base) * head_in[i, chunk(r)].astype(f32)
        bagg_out[chunk(r)] = total.astype(bf16)

        def send_down(to, _, r=r):
            z_copy(1, bagg_out, bagg_in, r, z, to).start()
            return _

        lax.fori_loop(0, z, send_down, 0)
        run = jnp.zeros((rows, HD), f32)
        suf_ref[heads - 1, chunk(r)] = run
        for i in range(heads - 2, -1, -1):
            begin = start_of(base + i + 1)
            if i + 2 < heads:
                run = flag(start_of(base + i + 2) <= base + i) * run
            run = flag(begin <= base + i) * (run + head_in[i + 1, chunk(r)].astype(f32))
            suf_ref[i, chunk(r)] = run

    lax.fori_loop(heads // 2, heads, local_backward, 0)

    open_after = jnp.where(z < planes - 1, start_of(after), groups)
    for r in range(CHUNKS):

        def join_back(at, total, r=r):
            z_copy(1, bagg_out, bagg_in, r, at, at).wait_recv()
            return total + flag(start_of(at * heads) <= base + heads - 1) * bagg_in[at, chunk(r)].astype(f32)

        total = lax.fori_loop(z + 1, planes, join_back, jnp.zeros((rows, HD), f32))
        for d in range(1, heads + 1):
            i = plane_peer(d)
            state = (suf_ref[i, chunk(r)] + flag(open_after <= base + i) * total).astype(bf16)
            if d < heads:
                back_out[i, chunk(r)] = state
                plane_start(3, back_out, back_in, r, i)
            else:
                back_in[p, chunk(r)] = state

    for d in range(heads):
        h = plane_peer(d)
        if d > 0:
            for r in range(CHUNKS):
                plane_wait(3, back_out, back_in, r, h)
        last = last_ref[...]
        gk_ref[:, lanes(h)] = (gk_acc[:, lanes(h)] + dot(v_ref[:, lanes(h)] * last, back_in[h], NT)).astype(bf16)
        gv_ref[:, lanes(h)] = (gv_acc[:, lanes(h)] + dot(k_ref[:, lanes(h)] * last, back_in[h], NN)).astype(bf16)

    for r in range(CHUNKS):

        def sent_up(to, _, r=r):
            z_copy(0, agg_out, agg_in, r, to, to).wait_send()
            return _

        def sent_down(to, _, r=r):
            z_copy(1, bagg_out, bagg_in, r, to, to).wait_send()
            return _

        lax.fori_loop(z + 1, planes, sent_up, 0)
        lax.fori_loop(0, z, sent_down, 0)


def write(a, b, c, d, a_out, b_out, c_out, d_out, sem):
    copies = [
        pltpu.make_async_copy(src, dst, sem.at[i])
        for i, (src, dst) in enumerate(((a, a_out), (b, b_out), (c, c_out), (d, d_out)))
    ]
    for copy in copies:
        copy.start()
    for copy in copies:
        copy.wait()


def solution(mesh):
    groups, spread = mesh.shape["seq"], mesh.shape["head"]

    def local(query_in, key_in, value_in, out_grad, norm_gain, doc_ids, start_group):
        tokens, columns = query_in.shape
        heads = columns // HD
        planes = groups // heads
        vmem = pl.BlockSpec(memory_space=pltpu.VMEM)
        state = pltpu.VMEM((heads, HD, HD), bf16)
        state_f = pltpu.VMEM((heads, HD, HD), f32)
        one = pltpu.VMEM((HD, HD), bf16)
        many = pltpu.VMEM((planes, HD, HD), bf16)
        row = pltpu.VMEM((tokens, HD), f32)
        scan = [state, state, state_f, one, many, state, state]
        outs = pl.pallas_call(
            functools.partial(kernel, planes, heads, spread, columns * spread),
            out_shape=[pltpu.VMEM((tokens, columns), bf16)] * 4,
            in_specs=[pl.BlockSpec(memory_space=pltpu.SMEM)] + [vmem] * 6,
            out_specs=[vmem] * 4,
            scratch_shapes=[
                pltpu.VMEM((tokens, tokens), f32),
                pltpu.VMEM((tokens, HD), bf16),
                pltpu.VMEM((tokens, HD), bf16),
                row,
                row,
                pltpu.VMEM((heads, tokens, tokens), bf16),
                pltpu.VMEM((tokens, columns), f32),
                pltpu.VMEM((tokens, columns), bf16),
                pltpu.VMEM((tokens, columns), f32),
                pltpu.VMEM((tokens, columns), f32),
                *scan,
                *scan,
                pltpu.VMEM((2, tokens), f32),
                pltpu.VMEM((spread, 2, tokens), f32),
                pltpu.SemaphoreType.DMA((4, CHUNKS, heads)),
                pltpu.SemaphoreType.DMA((4, CHUNKS, heads)),
                pltpu.SemaphoreType.DMA((2, CHUNKS, planes)),
                pltpu.SemaphoreType.DMA((2, CHUNKS, planes)),
                pltpu.SemaphoreType.DMA((spread,)),
                pltpu.SemaphoreType.DMA((spread,)),
            ],
            compiler_params=pltpu.CompilerParams(collective_id=0, has_side_effects=True),
            name="attention",
        )(
            start_group,
            doc_ids.reshape(1, tokens),
            query_in,
            key_in,
            value_in,
            out_grad,
            norm_gain.reshape(1, columns),
        )
        return pl.pallas_call(
            write,
            out_shape=[jax.ShapeDtypeStruct((tokens, columns), bf16)] * 4,
            in_specs=[vmem] * 4,
            out_specs=[pl.BlockSpec(memory_space=pl.ANY)] * 4,
            scratch_shapes=[pltpu.SemaphoreType.DMA((4,))],
            compiler_params=pltpu.CompilerParams(vmem_limit_bytes=1 << 20),
            name="write",
        )(*outs)

    wide = P("seq", "head")
    return jax.shard_map(
        local,
        mesh=mesh,
        in_specs=(wide, wide, wide, wide, P("head"), P("seq"), P()),
        out_specs=(wide, wide, wide, wide),
        check_vma=False,
    )
```

```python
import functools

import jax
import jax.numpy as jnp
from jax import lax
from jax.experimental import pallas as pl
from jax.experimental.pallas import tpu as pltpu
from jax.sharding import PartitionSpec as P

HD = 128
EPSILON = 1e-06
MESH = pl.DeviceIdType.MESH
f32, bf16 = jnp.float32, jnp.bfloat16


def dot(a, b, contract):
    return lax.dot_general(a, b, (contract, ((), ())), preferred_element_type=f32)


NN = ((1,), (0,))
NT = ((1,), (1,))
TN = ((0,), (0,))


def kernel(
    chips, ring, heads, spread, width,
    sg_ref, doc_ref, q_hbm, k_hbm, v_hbm, g_hbm, gain_ref,
    normed_ref, gq_ref, gk_ref, gv_ref,
    q_ref, k_ref, v_ref, g_ref,
    same_ref, first_ref, last_ref, inv_ref, coef_ref,
    weights_ref, att_ref, ga_ref, qf_ref, scaled_ref, gk_acc, gv_acc,
    pair_out, pair, sum_out, sum_in, run_out, run_in, share_out, carry_in,
    bpair_out, bpair, bsum_out, bsum_in, brun_out, brun_in, bshare_out, back_in,
    rows_out, rows_in,
    load_sem, chip_send, chip_recv, core_send, core_recv, x_send, x_recv,
):
    seq, col = lax.axis_index("seq"), lax.axis_index("head")
    chip, core = lax.div(seq, 2), lax.rem(seq, 2)
    partner = seq + 1 - 2 * core
    tokens = q_ref.shape[0]
    half = heads // 2
    piece = sum_out.shape[1]
    pieces = HD // piece
    mine, theirs = core * half, (1 - core) * half
    c0, c1, groups = 2 * chip, 2 * chip + 1, 2 * chips
    c2 = jnp.minimum(c0 + 2, groups - 1)
    lines = chips // ring

    loads = [
        pltpu.make_async_copy(src, dst, load_sem.at[i])
        for i, (src, dst) in enumerate(((k_hbm, k_ref), (v_hbm, v_ref), (q_hbm, q_ref), (g_hbm, g_ref)))
    ]
    for load in loads:
        load.start()

    def hops(offset, size):
        return min(offset, size - offset)

    offsets = sorted(
        ((dz, dy) for dz in range(lines) for dy in range(ring) if dz or dy),
        key=lambda o: -(hops(o[0], lines) + hops(o[1], ring)),
    )
    chip_z, chip_y = lax.div(chip, ring), lax.rem(chip, ring)
    others = [lax.rem(chip_z + dz, lines) * ring + lax.rem(chip_y + dy, ring) for dz, dy in offsets]

    barrier = pltpu.get_barrier_semaphore()
    for other in others:
        pl.semaphore_signal(barrier, inc=1, device_id=(2 * other + core, col), device_id_type=MESH)
    for d in range(1, spread):
        pl.semaphore_signal(barrier, inc=1, device_id=(seq, lax.rem(col + d, spread)), device_id_type=MESH)
    pl.semaphore_signal(barrier, inc=1, device_id=(partner, col), device_id_type=MESH)

    def lanes(h):
        return pl.ds(pl.multiple_of(h * HD, HD), HD)

    def flag(condition):
        return jnp.where(condition, 1.0, 0.0).astype(f32)

    def core_copy(phase, src, dst, at_src, at_dst, slot):
        return pltpu.make_async_remote_copy(
            src_ref=src.at[at_src],
            dst_ref=dst.at[at_dst],
            send_sem=core_send.at[phase, slot],
            recv_sem=core_recv.at[phase, slot],
            device_id=(partner, col),
            device_id_type=MESH,
        )

    def chip_copy(phase, src, dst, at_src, at_dst, other):
        return pltpu.make_async_remote_copy(
            src_ref=src.at[at_src],
            dst_ref=dst.at[at_dst],
            send_sem=chip_send.at[phase, at_src],
            recv_sem=chip_recv.at[phase, at_dst],
            device_id=(2 * other + core, col),
            device_id_type=MESH,
        )

    def chip_start(phase, src, dst):
        for other in others:
            chip_copy(phase, src, dst, other, chip, other).start()

    def chip_wait(phase, src, dst):
        def one(d, carry):
            other = lax.rem(chip + d, chips)
            chip_copy(phase, src, dst, other, other, other).wait_recv()
            return carry

        lax.fori_loop(1, chips, one, 0)

    def chip_sent(phase, src, dst):
        def one(d, carry):
            other = lax.rem(chip + d, chips)
            chip_copy(phase, src, dst, other, other, other).wait_send()
            return carry

        lax.fori_loop(1, chips, one, 0)

    def put(ref, j, state):
        ref[pl.ds(j * pieces, pieces)] = state.astype(bf16).reshape(pieces, piece, HD)

    def take(ref, j):
        return ref[pl.ds(j * pieces, pieces)].reshape(HD, HD).astype(f32)

    doc_row = jnp.broadcast_to(doc_ref[...].astype(f32), (tokens, tokens))
    doc_col = doc_row.T
    causal = lax.broadcasted_iota(jnp.int32, (tokens, tokens), 0) >= lax.broadcasted_iota(
        jnp.int32, (tokens, tokens), 1
    )
    same_ref[...] = jnp.where(causal & (doc_row == doc_col), 1.0, 0.0)
    own = doc_col[:, :HD]
    first_ref[...] = jnp.where(own == own[:1], 1.0, 0.0).astype(bf16)
    last_ref[...] = jnp.where(own == own[tokens - 1 :], 1.0, 0.0).astype(bf16)

    loads[0].wait()
    loads[1].wait()
    for j in range(half):
        at = lanes(theirs + j)
        pair_out[j] = dot(k_ref[:, at] * last_ref[...], v_ref[:, at], TN)
    pl.semaphore_wait(barrier, chips + spread - 1)
    for j in range(half):
        core_copy(0, pair_out, pair.at[core], j, j, j).start()
    for j in range(half):
        at = lanes(mine + j)
        pair[core, j] = dot(k_ref[:, at] * last_ref[...], v_ref[:, at], TN)

    both = flag(sg_ref[c2] <= c0)
    for j in range(half):
        core_copy(0, pair_out, pair.at[1 - core], j, j, j).wait_recv()
        put(sum_out, j, pair[1, j] + both * pair[0, j])
    sum_in[chip] = sum_out[chip]
    chip_start(0, sum_out, sum_in)

    loads[2].wait()
    loads[3].wait()

    def local_forward(h, _):
        at = lanes(h)
        scores = dot(q_ref[:, at], k_ref[:, at], NT)
        weights = jnp.where(same_ref[...] > 0.5, scores, 0.0).astype(bf16)
        weights_ref[h] = weights
        att_ref[:, at] = dot(weights, v_ref[:, at], NN)
        qf_ref[:, at] = q_ref[:, at] * first_ref[...]
        scaled_ref[:, at] = gain_ref[:, at] * g_ref[:, at].astype(f32)
        return _

    lax.fori_loop(0, heads, local_forward, 0)

    chip_wait(0, sum_out, sum_in)
    run = jnp.zeros((piece, HD), f32)
    run_out[0] = run.astype(bf16)
    for w in range(1, chips):
        begin = sg_ref[2 * w]
        run = flag(begin <= 2 * w - 1) * (sum_in[w - 1].astype(f32) + flag(begin < 2 * w - 2) * run)
        run_out[w] = run.astype(bf16)
    run_in[chip] = run_out[chip]
    chip_start(1, run_out, run_in)
    chip_wait(1, run_out, run_in)

    odd = core == 1
    inside, through = flag(sg_ref[c1] <= c0), flag(sg_ref[c1] < c0)
    own_a, own_b = jnp.where(odd, inside, 0.0), jnp.where(odd, through, 1.0)
    their_a, their_b = jnp.where(odd, 0.0, inside), jnp.where(odd, 1.0, through)
    for j in range(half):
        share_out[j] = (their_a * pair[0, j] + their_b * take(run_in, j)).astype(bf16)
        core_copy(1, share_out, carry_in, j, mine + j, j).start()
    for j in range(half):
        carry_in[mine + j] = (own_a * pair[0, j] + own_b * take(run_in, j)).astype(bf16)

    square = jnp.zeros((tokens, HD), f32)
    cross = jnp.zeros((tokens, HD), f32)
    for i in range(heads):
        j = i % half
        h = mine + j if i < half else theirs + j
        at = lanes(h)
        if i >= half:
            core_copy(1, share_out, carry_in, j, h, j).wait_recv()
        att = att_ref[:, at] + dot(qf_ref[:, at], carry_in[h], NN)
        att_ref[:, at] = att
        square = square + att * att
        cross = cross + scaled_ref[:, at] * att
    rows_out[0:1] = jnp.sum(square.T, axis=0, keepdims=True)
    rows_out[1:2] = jnp.sum(cross.T, axis=0, keepdims=True)

    def x_copy(at_dst, peer):
        return pltpu.make_async_remote_copy(
            src_ref=rows_out,
            dst_ref=rows_in.at[at_dst],
            send_sem=x_send.at[peer],
            recv_sem=x_recv.at[at_dst],
            device_id=(seq, peer),
            device_id_type=MESH,
        )

    for d in range(1, spread):
        x_copy(col, lax.rem(col + d, spread)).start()
    sums = rows_out[...]
    for d in range(1, spread):
        peer = lax.rem(col + d, spread)
        x_copy(peer, peer).wait_recv()
        sums = sums + rows_in[peer]
    inverse = lax.rsqrt(sums[0:1] / width + EPSILON)
    coef = inverse * inverse * inverse * sums[1:2] / width
    inv_ref[...] = jnp.broadcast_to(inverse, (HD, tokens)).T
    coef_ref[...] = jnp.broadcast_to(coef, (HD, tokens)).T

    for i in range(heads):
        j = i % half
        h = theirs + j if i < half else mine + j
        at = lanes(h)
        ga = (inv_ref[...] * scaled_ref[:, at] - coef_ref[...] * att_ref[:, at]).astype(bf16)
        ga_ref[:, at] = ga
        state = dot(qf_ref[:, at], ga, TN)
        if i < half:
            bpair_out[j] = state
            core_copy(2, bpair_out, bpair.at[core], j, j, j).start()
        else:
            bpair[core, j] = state

    from_first, from_second = flag(sg_ref[c0] < c0), flag(sg_ref[c1] < c0)
    for j in range(half):
        core_copy(2, bpair_out, bpair.at[1 - core], j, j, j).wait_recv()
        put(bsum_out, j, from_first * bpair[0, j] + from_second * bpair[1, j])
    bsum_in[chip] = bsum_out[chip]
    chip_start(2, bsum_out, bsum_in)

    def local_backward(h, _):
        at = lanes(h)
        ga = ga_ref[:, at]
        normed_ref[:, at] = (att_ref[:, at] * inv_ref[...] * gain_ref[:, at]).astype(bf16)
        scores = dot(ga, v_ref[:, at], NT)
        scores = jnp.where(same_ref[...] > 0.5, scores, 0.0).astype(bf16)
        part = dot(ga * first_ref[...], carry_in[h], NT)
        gq_ref[:, at] = (dot(scores, k_ref[:, at], NN) + part).astype(bf16)
        gk_acc[:, at] = dot(scores, q_ref[:, at], TN)
        gv_acc[:, at] = dot(weights_ref[h], ga, TN)
        return _

    lax.fori_loop(0, half, local_backward, 0)

    chip_wait(2, bsum_out, bsum_in)
    run = jnp.zeros((piece, HD), f32)
    brun_out[chips - 1] = run.astype(bf16)
    for w in range(chips - 2, -1, -1):
        run = flag(sg_ref[min(2 * w + 4, groups - 1)] <= 2 * w + 1) * run
        run = flag(sg_ref[2 * w + 2] <= 2 * w + 1) * (bsum_in[w + 1].astype(f32) + run)
        brun_out[w] = run.astype(bf16)
    brun_in[chip] = brun_out[chip]
    chip_start(3, brun_out, brun_in)

    lax.fori_loop(half, heads, local_backward, 0)

    chip_wait(3, brun_out, brun_in)
    reach = flag(sg_ref[c2] <= c0)
    own_a, own_b = jnp.where(odd, 0.0, inside), jnp.where(odd, 1.0, reach)
    their_a, their_b = jnp.where(odd, inside, 0.0), jnp.where(odd, reach, 1.0)
    for j in range(half):
        bshare_out[j] = (their_a * bpair[1, j] + their_b * take(brun_in, j)).astype(bf16)
        core_copy(3, bshare_out, back_in, j, mine + j, j).start()
    for j in range(half):
        back_in[mine + j] = (own_a * bpair[1, j] + own_b * take(brun_in, j)).astype(bf16)

    for i in range(heads):
        j = i % half
        h = mine + j if i < half else theirs + j
        at = lanes(h)
        if i >= half:
            core_copy(3, bshare_out, back_in, j, h, j).wait_recv()
        last = last_ref[...]
        gk_ref[:, at] = (gk_acc[:, at] + dot(v_ref[:, at] * last, back_in[h], NT)).astype(bf16)
        gv_ref[:, at] = (gv_acc[:, at] + dot(k_ref[:, at] * last, back_in[h], NN)).astype(bf16)

    for phase, src, dst in ((0, sum_out, sum_in), (1, run_out, run_in), (2, bsum_out, bsum_in), (3, brun_out, brun_in)):
        chip_sent(phase, src, dst)
    for j in range(half):
        core_copy(0, pair_out, pair.at[core], j, j, j).wait_send()
        core_copy(1, share_out, carry_in, j, mine + j, j).wait_send()
        core_copy(2, bpair_out, bpair.at[core], j, j, j).wait_send()
        core_copy(3, bshare_out, back_in, j, mine + j, j).wait_send()
    for d in range(1, spread):
        peer = lax.rem(col + d, spread)
        x_copy(col, peer).wait_send()


def write(a, b, c, d, a_out, b_out, c_out, d_out, sem):
    copies = [
        pltpu.make_async_copy(src, dst, sem.at[i])
        for i, (src, dst) in enumerate(((a, a_out), (b, b_out), (c, c_out), (d, d_out)))
    ]
    for copy in copies:
        copy.start()
    for copy in copies:
        copy.wait()


def solution(mesh):
    groups, spread = mesh.shape["seq"], mesh.shape["head"]
    chips = groups // 2
    ring = 4 if chips % 4 == 0 else 1

    def local(query_in, key_in, value_in, out_grad, norm_gain, doc_ids, start_group):
        tokens, columns = query_in.shape
        heads = columns // HD
        half = heads // 2
        vmem = pl.BlockSpec(memory_space=pltpu.VMEM)
        hbm = pl.BlockSpec(memory_space=pltpu.HBM)
        states = pltpu.VMEM((half, HD, HD), f32)
        pair = pltpu.VMEM((2, half, HD, HD), f32)
        pieces = pltpu.VMEM((chips, half * HD // chips, HD), bf16)
        narrow = pltpu.VMEM((tokens, HD), bf16)
        row = pltpu.VMEM((tokens, HD), f32)
        wide_b = pltpu.VMEM((tokens, columns), bf16)
        wide_f = pltpu.VMEM((tokens, columns), f32)
        scan = [states, pair, pieces, pieces, pieces, pieces]
        scan += [pltpu.VMEM((half, HD, HD), bf16), pltpu.VMEM((heads, HD, HD), bf16)]
        outs = pl.pallas_call(
            functools.partial(kernel, chips, ring, heads, spread, columns * spread),
            out_shape=[pltpu.VMEM((tokens, columns), bf16)] * 4,
            in_specs=[pl.BlockSpec(memory_space=pltpu.SMEM), vmem] + [hbm] * 4 + [vmem],
            out_specs=[vmem] * 4,
            scratch_shapes=[
                *[wide_b] * 4,
                pltpu.VMEM((tokens, tokens), f32),
                narrow,
                narrow,
                row,
                row,
                pltpu.VMEM((heads, tokens, tokens), bf16),
                wide_f,
                wide_b,
                wide_b,
                wide_f,
                wide_f,
                wide_f,
                *scan,
                *scan,
                pltpu.VMEM((2, tokens), f32),
                pltpu.VMEM((spread, 2, tokens), f32),
                pltpu.SemaphoreType.DMA((4,)),
                pltpu.SemaphoreType.DMA((4, chips)),
                pltpu.SemaphoreType.DMA((4, chips)),
                pltpu.SemaphoreType.DMA((4, half)),
                pltpu.SemaphoreType.DMA((4, half)),
                pltpu.SemaphoreType.DMA((spread,)),
                pltpu.SemaphoreType.DMA((spread,)),
            ],
            compiler_params=pltpu.CompilerParams(collective_id=0, has_side_effects=True),
            name="attention",
        )(
            start_group,
            doc_ids.reshape(1, tokens),
            query_in,
            key_in,
            value_in,
            out_grad,
            norm_gain.reshape(1, columns),
        )
        return pl.pallas_call(
            write,
            out_shape=[jax.ShapeDtypeStruct((tokens, columns), bf16)] * 4,
            in_specs=[vmem] * 4,
            out_specs=[pl.BlockSpec(memory_space=pl.ANY)] * 4,
            scratch_shapes=[pltpu.SemaphoreType.DMA((4,))],
            compiler_params=pltpu.CompilerParams(vmem_limit_bytes=1 << 20),
            name="write",
        )(*outs)

    wide = P("seq", "head")
    return jax.shard_map(
        local,
        mesh=mesh,
        in_specs=(wide, wide, wide, wide, P("head"), P("seq"), P()),
        out_specs=(wide, wide, wide, wide),
        check_vma=False,
    )
```

```python
import functools

import jax
import jax.numpy as jnp
from jax import lax
from jax.experimental import pallas as pl
from jax.experimental.pallas import tpu as pltpu
from jax.sharding import PartitionSpec as P

HD = 128
EPSILON = 1e-06
MESH = pl.DeviceIdType.MESH
f32, bf16 = jnp.float32, jnp.bfloat16


def dot(a, b, contract):
    return lax.dot_general(a, b, (contract, ((), ())), preferred_element_type=f32)


NN = ((1,), (0,))
NT = ((1,), (1,))
TN = ((0,), (0,))


def kernel(
    chips, ring, heads, spread, width,
    sg_ref, doc_ref, q_hbm, k_hbm, v_hbm, g_hbm, gain_ref,
    normed_ref, gq_ref, gk_acc, gv_acc, kl_ref, vl_ref, back_in,
    q_ref, k_ref, v_ref, g_ref,
    same_ref, first_ref, last_ref, inv_ref, coef_ref,
    weights_ref, att_ref, ga_ref, qf_ref, qt_ref, scaled_ref,
    pair_out, pair, sum_out, sum_in, run_out, run_in, share_out, carry_in,
    bpair_out, bpair, bsum_out, bsum_in, brun_out, brun_in, bshare_out,
    rows_out, rows_in,
    load_sem, chip_send, chip_recv, core_send, core_recv, x_send, x_recv, here, go,
):
    seq, col = lax.axis_index("seq"), lax.axis_index("head")
    chip, core = lax.div(seq, 2), lax.rem(seq, 2)
    partner = seq + 1 - 2 * core
    tokens = q_ref.shape[0]
    half = heads // 2
    piece = sum_out.shape[1]
    pieces = HD // piece
    mine, theirs = core * half, (1 - core) * half
    c0, c1, groups = 2 * chip, 2 * chip + 1, 2 * chips
    c2 = jnp.minimum(c0 + 2, groups - 1)
    lines = chips // ring

    loads = [
        pltpu.make_async_copy(src, dst, load_sem.at[i])
        for i, (src, dst) in enumerate(((k_hbm, k_ref), (v_hbm, v_ref), (q_hbm, q_ref), (g_hbm, g_ref)))
    ]
    for load in loads:
        load.start()

    def hops(offset, size):
        return min(offset, size - offset)

    offsets = sorted(
        ((dz, dy) for dz in range(lines) for dy in range(ring) if dz or dy),
        key=lambda o: -(hops(o[0], lines) + hops(o[1], ring)),
    )
    chip_z, chip_y = lax.div(chip, ring), lax.rem(chip, ring)
    others = [lax.rem(chip_z + dz, lines) * ring + lax.rem(chip_y + dy, ring) for dz, dy in offsets]

    barrier = pltpu.get_barrier_semaphore()

    @pl.when(core == 0)
    def _():
        pl.semaphore_signal(barrier, inc=1, device_id=(partner, col), device_id_type=MESH)

    for other in others:
        pl.semaphore_signal(barrier, inc=1, device_id=(2 * other, col), device_id_type=MESH)
    for d in range(1, spread):
        pl.semaphore_signal(barrier, inc=1, device_id=(c0, lax.rem(col + d, spread)), device_id_type=MESH)

    def lanes(h):
        return pl.ds(pl.multiple_of(h * HD, HD), HD)

    def flag(condition):
        return jnp.where(condition, 1.0, 0.0).astype(f32)

    def core_copy(phase, src, dst, at_src, at_dst, slot):
        return pltpu.make_async_remote_copy(
            src_ref=src.at[at_src],
            dst_ref=dst.at[at_dst],
            send_sem=core_send.at[phase, slot],
            recv_sem=core_recv.at[phase, slot],
            device_id=(partner, col),
            device_id_type=MESH,
        )

    def chip_copy(phase, src, dst, at_src, at_dst, other):
        return pltpu.make_async_remote_copy(
            src_ref=src.at[at_src],
            dst_ref=dst.at[at_dst],
            send_sem=chip_send.at[phase],
            recv_sem=chip_recv.at[phase],
            device_id=(2 * other + core, col),
            device_id_type=MESH,
        )

    def chip_start(phase, src, dst):
        for other in others:
            chip_copy(phase, src, dst, other, chip, other).start()

    every = pl.ds(0, chips - 1)

    def chip_wait(phase, src, dst):
        chip_copy(phase, src, dst, every, every, others[0]).wait_recv()

    def chip_sent(phase, src, dst):
        chip_copy(phase, src, dst, every, every, others[0]).wait_send()

    def put(ref, j, state):
        ref[pl.ds(j * pieces, pieces)] = state.astype(bf16).reshape(pieces, piece, HD)

    def take(ref, j):
        return ref[pl.ds(j * pieces, pieces)].reshape(HD, HD).astype(f32)

    docs = doc_ref[...].astype(f32)
    last_row = jnp.where(docs == docs[:, tokens - 1 :], 1.0, 0.0).astype(bf16)
    first_row = jnp.where(docs == docs[:, :1], 1.0, 0.0).astype(bf16)

    def tail(h):
        at = lanes(h)
        return dot(k_ref[:, at].T * last_row, v_ref[:, at], NN)

    loads[0].wait()
    loads[1].wait()
    for j in range(half):
        pair_out[j] = tail(theirs + j)

    @pl.when(core == 1)
    def _():
        pl.semaphore_wait(barrier, 1)
        pl.semaphore_signal(here, inc=1, device_id=(partner, col), device_id_type=MESH)

    @pl.when(core == 0)
    def _():
        pl.semaphore_wait(here, 1)

    for j in range(half):
        core_copy(0, pair_out, pair.at[core], j, j, j).start()
    for j in range(half):
        pair[core, j] = tail(mine + j)

    both = flag(sg_ref[c2] <= c0)
    for j in range(half):
        core_copy(0, pair_out, pair.at[1 - core], j, j, j).wait_recv()
        put(sum_out, j, pair[1, j] + both * pair[0, j])
    sum_in[chip] = sum_out[chip]

    @pl.when(core == 0)
    def _():
        pl.semaphore_wait(barrier, 2 * (chips - 1) + 2 * (spread - 1))
        pl.semaphore_signal(go, inc=1, device_id=(partner, col), device_id_type=MESH)

    @pl.when(core == 1)
    def _():
        pl.semaphore_wait(go, 1)

    chip_start(0, sum_out, sum_in)

    doc_row = jnp.broadcast_to(docs, (tokens, tokens))
    doc_col = doc_row.T
    causal = lax.broadcasted_iota(jnp.int32, (tokens, tokens), 0) >= lax.broadcasted_iota(
        jnp.int32, (tokens, tokens), 1
    )
    same_ref[...] = jnp.where(causal & (doc_row == doc_col), 1.0, 0.0)
    own = doc_col[:, :HD]
    first_ref[...] = jnp.where(own == own[:1], 1.0, 0.0).astype(bf16)
    last_ref[...] = jnp.where(own == own[tokens - 1 :], 1.0, 0.0).astype(bf16)
    loads[2].wait()
    loads[3].wait()

    def local_forward(h, _):
        at = lanes(h)
        scores = dot(q_ref[:, at], k_ref[:, at], NT)
        weights = jnp.where(same_ref[...] > 0.5, scores, 0.0).astype(bf16)
        weights_ref[h] = weights
        att_ref[:, at] = dot(weights, v_ref[:, at], NN)
        qf_ref[:, at] = q_ref[:, at] * first_ref[...]
        qt_ref[h] = q_ref[:, at].T * first_row
        kl_ref[:, at] = k_ref[:, at] * last_ref[...]
        vl_ref[:, at] = v_ref[:, at] * last_ref[...]
        scaled_ref[:, at] = gain_ref[:, at] * g_ref[:, at].astype(f32)
        return _

    lax.fori_loop(0, heads, local_forward, 0)

    chip_wait(0, sum_out, sum_in)
    run = jnp.zeros((piece, HD), f32)
    run_out[0] = run.astype(bf16)
    for w in range(1, chips):
        begin = sg_ref[2 * w]
        run = flag(begin <= 2 * w - 1) * (sum_in[w - 1].astype(f32) + flag(begin < 2 * w - 2) * run)
        run_out[w] = run.astype(bf16)
    run_in[chip] = run_out[chip]
    chip_start(1, run_out, run_in)
    chip_wait(1, run_out, run_in)

    odd = core == 1
    inside, through = flag(sg_ref[c1] <= c0), flag(sg_ref[c1] < c0)
    own_a, own_b = jnp.where(odd, inside, 0.0), jnp.where(odd, through, 1.0)
    their_a, their_b = jnp.where(odd, 0.0, inside), jnp.where(odd, 1.0, through)
    for j in range(half):
        share_out[j] = (their_a * pair[0, j] + their_b * take(run_in, j)).astype(bf16)
        core_copy(1, share_out, carry_in, j, mine + j, j).start()
    for j in range(half):
        carry_in[mine + j] = (own_a * pair[0, j] + own_b * take(run_in, j)).astype(bf16)

    square = jnp.zeros((tokens, HD), f32)
    cross = jnp.zeros((tokens, HD), f32)
    for i in range(heads):
        j = i % half
        h = mine + j if i < half else theirs + j
        at = lanes(h)
        if i >= half:
            core_copy(1, share_out, carry_in, j, h, j).wait_recv()
        att = att_ref[:, at] + dot(qf_ref[:, at], carry_in[h], NN)
        att_ref[:, at] = att
        square = square + att * att
        cross = cross + scaled_ref[:, at] * att
    rows_out[0:1] = jnp.sum(square.T, axis=0, keepdims=True)
    rows_out[1:2] = jnp.sum(cross.T, axis=0, keepdims=True)

    def x_copy(at_dst, peer):
        return pltpu.make_async_remote_copy(
            src_ref=rows_out,
            dst_ref=rows_in.at[at_dst],
            send_sem=x_send.at[peer],
            recv_sem=x_recv.at[at_dst],
            device_id=(seq, peer),
            device_id_type=MESH,
        )

    for d in range(1, spread):
        x_copy(col, lax.rem(col + d, spread)).start()
    sums = rows_out[...]
    for d in range(1, spread):
        peer = lax.rem(col + d, spread)
        x_copy(peer, peer).wait_recv()
        sums = sums + rows_in[peer]
    inverse = lax.rsqrt(sums[0:1] / width + EPSILON)
    coef = inverse * inverse * inverse * sums[1:2] / width
    inv_ref[...] = jnp.broadcast_to(inverse, (HD, tokens)).T
    coef_ref[...] = jnp.broadcast_to(coef, (HD, tokens)).T

    for i in range(heads):
        j = i % half
        h = theirs + j if i < half else mine + j
        at = lanes(h)
        ga = (inv_ref[...] * scaled_ref[:, at] - coef_ref[...] * att_ref[:, at]).astype(bf16)
        ga_ref[:, at] = ga
        state = dot(qt_ref[h], ga, NN)
        if i < half:
            bpair_out[j] = state
            core_copy(2, bpair_out, bpair.at[core], j, j, j).start()
        else:
            bpair[core, j] = state

    from_first, from_second = flag(sg_ref[c0] < c0), flag(sg_ref[c1] < c0)
    for j in range(half):
        core_copy(2, bpair_out, bpair.at[1 - core], j, j, j).wait_recv()
        put(bsum_out, j, from_first * bpair[0, j] + from_second * bpair[1, j])
    bsum_in[chip] = bsum_out[chip]
    chip_start(2, bsum_out, bsum_in)

    def local_backward(h, _):
        at = lanes(h)
        ga = ga_ref[:, at]
        normed_ref[:, at] = (att_ref[:, at] * inv_ref[...] * gain_ref[:, at]).astype(bf16)
        scores = dot(ga, v_ref[:, at], NT)
        scores = jnp.where(same_ref[...] > 0.5, scores, 0.0).astype(bf16)
        part = dot(ga * first_ref[...], carry_in[h], NT)
        gq_ref[:, at] = (dot(scores, k_ref[:, at], NN) + part).astype(bf16)
        gk_acc[:, at] = dot(scores, q_ref[:, at], TN)
        gv_acc[:, at] = dot(weights_ref[h], ga, TN)
        return _

    lax.fori_loop(0, half, local_backward, 0)

    chip_wait(2, bsum_out, bsum_in)
    run = jnp.zeros((piece, HD), f32)
    brun_out[chips - 1] = run.astype(bf16)
    for w in range(chips - 2, -1, -1):
        run = flag(sg_ref[min(2 * w + 4, groups - 1)] <= 2 * w + 1) * run
        run = flag(sg_ref[2 * w + 2] <= 2 * w + 1) * (bsum_in[w + 1].astype(f32) + run)
        brun_out[w] = run.astype(bf16)
    brun_in[chip] = brun_out[chip]
    chip_start(3, brun_out, brun_in)

    lax.fori_loop(half, heads, local_backward, 0)

    chip_wait(3, brun_out, brun_in)
    reach = flag(sg_ref[c2] <= c0)
    own_a, own_b = jnp.where(odd, 0.0, inside), jnp.where(odd, 1.0, reach)
    their_a, their_b = jnp.where(odd, inside, 0.0), jnp.where(odd, reach, 1.0)
    for j in range(half):
        bshare_out[j] = (their_a * bpair[1, j] + their_b * take(brun_in, j)).astype(bf16)
        core_copy(3, bshare_out, back_in, j, mine + j, j).start()
    for j in range(half):
        back_in[mine + j] = (own_a * bpair[1, j] + own_b * take(brun_in, j)).astype(bf16)

    for j in range(half):
        core_copy(3, bshare_out, back_in, j, theirs + j, j).wait_recv()

    for phase, src, dst in ((0, sum_out, sum_in), (1, run_out, run_in), (2, bsum_out, bsum_in), (3, brun_out, brun_in)):
        chip_sent(phase, src, dst)
    for j in range(half):
        core_copy(0, pair_out, pair.at[core], j, j, j).wait_send()
        core_copy(1, share_out, carry_in, j, mine + j, j).wait_send()
        core_copy(2, bpair_out, bpair.at[core], j, j, j).wait_send()
        core_copy(3, bshare_out, back_in, j, mine + j, j).wait_send()
    for d in range(1, spread):
        peer = lax.rem(col + d, spread)
        x_copy(col, peer).wait_send()


def finish(
    normed_ref, gq_ref, gk_acc, gv_acc, kl_ref, vl_ref, back_ref,
    normed_out, gq_out, gk_out, gv_out,
    gk_ref, gv_ref, sem,
):
    heads = back_ref.shape[0]
    copies = [
        pltpu.make_async_copy(normed_ref, normed_out, sem.at[0]),
        pltpu.make_async_copy(gq_ref, gq_out, sem.at[1]),
    ]
    for copy in copies:
        copy.start()
    for h in range(heads):
        at = slice(h * HD, (h + 1) * HD)
        gk_ref[:, at] = (gk_acc[:, at] + dot(vl_ref[:, at], back_ref[h], NT)).astype(bf16)
        gv_ref[:, at] = (gv_acc[:, at] + dot(kl_ref[:, at], back_ref[h], NN)).astype(bf16)
        if h % 2 == 1:
            done = pl.ds((h - 1) * HD, 2 * HD)
            for i, (src, dst) in enumerate(((gk_ref, gk_out), (gv_ref, gv_out))):
                copy = pltpu.make_async_copy(src.at[:, done], dst.at[:, done], sem.at[h + 1 + i])
                copy.start()
                copies.append(copy)
    for copy in copies:
        copy.wait()


def solution(mesh):
    groups, spread = mesh.shape["seq"], mesh.shape["head"]
    chips = groups // 2
    ring = 4 if chips % 4 == 0 else 1

    def local(query_in, key_in, value_in, out_grad, norm_gain, doc_ids, start_group):
        tokens, columns = query_in.shape
        heads = columns // HD
        half = heads // 2
        vmem = pl.BlockSpec(memory_space=pltpu.VMEM)
        hbm = pl.BlockSpec(memory_space=pltpu.HBM)
        states = pltpu.VMEM((half, HD, HD), f32)
        pair = pltpu.VMEM((2, half, HD, HD), f32)
        pieces = pltpu.VMEM((chips, half * HD // chips, HD), bf16)
        narrow = pltpu.VMEM((tokens, HD), bf16)
        row = pltpu.VMEM((tokens, HD), f32)
        wide_b = pltpu.VMEM((tokens, columns), bf16)
        wide_f = pltpu.VMEM((tokens, columns), f32)
        scan = [states, pair, pieces, pieces, pieces, pieces]
        scan += [pltpu.VMEM((half, HD, HD), bf16)]
        outs = pl.pallas_call(
            functools.partial(kernel, chips, ring, heads, spread, columns * spread),
            out_shape=[wide_b, wide_b, wide_f, wide_f, wide_b, wide_b, pltpu.VMEM((heads, HD, HD), bf16)],
            in_specs=[pl.BlockSpec(memory_space=pltpu.SMEM), vmem] + [hbm] * 4 + [vmem],
            out_specs=[vmem] * 7,
            scratch_shapes=[
                *[wide_b] * 4,
                pltpu.VMEM((tokens, tokens), f32),
                narrow,
                narrow,
                row,
                row,
                pltpu.VMEM((heads, tokens, tokens), bf16),
                wide_f,
                wide_b,
                wide_b,
                pltpu.VMEM((heads, HD, tokens), bf16),
                wide_f,
                *scan,
                pltpu.VMEM((heads, HD, HD), bf16),
                *scan,
                pltpu.VMEM((2, tokens), f32),
                pltpu.VMEM((spread, 2, tokens), f32),
                pltpu.SemaphoreType.DMA((4,)),
                pltpu.SemaphoreType.DMA((4,)),
                pltpu.SemaphoreType.DMA((4,)),
                pltpu.SemaphoreType.DMA((4, half)),
                pltpu.SemaphoreType.DMA((4, half)),
                pltpu.SemaphoreType.DMA((spread,)),
                pltpu.SemaphoreType.DMA((spread,)),
                pltpu.SemaphoreType.REGULAR,
                pltpu.SemaphoreType.REGULAR,
            ],
            compiler_params=pltpu.CompilerParams(
                collective_id=0, has_side_effects=True, vmem_limit_bytes=62_300_000
            ),
            name="attention",
        )(
            start_group,
            doc_ids.reshape(1, tokens),
            query_in,
            key_in,
            value_in,
            out_grad,
            norm_gain.reshape(1, columns),
        )
        return pl.pallas_call(
            finish,
            out_shape=[jax.ShapeDtypeStruct((tokens, columns), bf16)] * 4,
            in_specs=[vmem] * 7,
            out_specs=[pl.BlockSpec(memory_space=pl.ANY)] * 4,
            scratch_shapes=[wide_b, wide_b, pltpu.SemaphoreType.DMA((heads + 2,))],
            compiler_params=pltpu.CompilerParams(vmem_limit_bytes=4 << 20),
            name="finish",
        )(*outs)

    wide = P("seq", "head")
    return jax.shard_map(
        local,
        mesh=mesh,
        in_specs=(wide, wide, wide, wide, P("head"), P("seq"), P()),
        out_specs=(wide, wide, wide, wide),
        check_vma=False,
    )
```

```python
import functools

import jax
import jax.numpy as jnp
from jax import lax
from jax.experimental import pallas as pl
from jax.experimental.pallas import tpu as pltpu
from jax.sharding import PartitionSpec as P

HD = 128
EPSILON = 1e-06
MESH = pl.DeviceIdType.MESH
f32, bf16 = jnp.float32, jnp.bfloat16


def dot(a, b, contract):
    return lax.dot_general(a, b, (contract, ((), ())), preferred_element_type=f32)


NN = ((1,), (0,))
NT = ((1,), (1,))
TN = ((0,), (0,))


def kernel(
    chips, ring, heads, spread, width,
    sg_ref, doc_ref, q_hbm, k_hbm, v_hbm, g_hbm, gain_ref,
    normed_ref, gq_ref, gk_acc, gv_acc, kl_ref, vl_ref, back_in,
    q_ref, k_ref, v_ref, g_ref, doc_in, kx_ref, vx_ref,
    same_ref, first_ref, last_ref, inv_ref, coef_ref,
    weights_ref, att_ref, ga_ref, qf_ref, qt_ref, scaled_ref,
    pair, sum_out, sum_in, run_out, run_in, carry_ref,
    bpair, bsum_out, bsum_in, brun_out, brun_in, bshare_out,
    rows_out, rows_in, normed_out, gq_out, gk_out, gv_out,
    load_sem, chip_send, chip_recv, in_send, in_recv, out_send, out_recv, core_send, core_recv,
    x_send, x_recv, here, go,
):
    seq, col = lax.axis_index("seq"), lax.axis_index("head")
    chip, core = lax.div(seq, 2), lax.rem(seq, 2)
    partner = seq + 1 - 2 * core
    tokens = q_ref.shape[1]
    half = heads // 2
    piece = sum_out.shape[1]
    pieces = HD // piece
    mine, theirs = core * half, (1 - core) * half
    c0, c1, groups = 2 * chip, 2 * chip + 1, 2 * chips
    c2 = jnp.minimum(c0 + 2, groups - 1)
    lines = chips // ring
    block = (core, 1 - core)

    def columns(first):
        return pl.ds(pl.multiple_of(first * HD, HD), half * HD)

    loads = [
        pltpu.make_async_copy(src.at[:, columns(first)], dst, load_sem.at[i])
        for i, (src, first, dst) in enumerate(
            (
                (k_hbm, mine, k_ref.at[0]),
                (v_hbm, mine, v_ref.at[0]),
                (q_hbm, mine, q_ref.at[0]),
                (g_hbm, mine, g_ref.at[0]),
                (k_hbm, theirs, kx_ref),
                (v_hbm, theirs, vx_ref),
            )
        )
    ]
    loads[0].start()
    loads[1].start()

    def hops(offset, size):
        return min(offset, size - offset)

    offsets = sorted(
        ((dz, dy) for dz in range(lines) for dy in range(ring) if dz or dy),
        key=lambda o: -(hops(o[0], lines) + hops(o[1], ring)),
    )
    chip_z, chip_y = lax.div(chip, ring), lax.rem(chip, ring)
    others = [lax.rem(chip_z + dz, lines) * ring + lax.rem(chip_y + dy, ring) for dz, dy in offsets]

    barrier = pltpu.get_barrier_semaphore()

    @pl.when(core == 0)
    def _():
        pl.semaphore_signal(barrier, inc=1, device_id=(partner, col), device_id_type=MESH)

    for other in others:
        pl.semaphore_signal(barrier, inc=1, device_id=(2 * other, col), device_id_type=MESH)
    for d in range(1, spread):
        pl.semaphore_signal(barrier, inc=1, device_id=(c0, lax.rem(col + d, spread)), device_id_type=MESH)

    def lanes(h):
        return pl.ds(pl.multiple_of(h * HD, HD), HD)

    def flag(condition):
        return jnp.where(condition, 1.0, 0.0).astype(f32)

    def to_partner(src, dst, send, recv):
        return pltpu.make_async_remote_copy(
            src_ref=src, dst_ref=dst, send_sem=send, recv_sem=recv, device_id=(partner, col), device_id_type=MESH
        )

    ins = [
        to_partner(src, dst, in_send.at[i], in_recv.at[i])
        for i, (src, dst) in enumerate(
            (
                (doc_ref, doc_in),
                (k_hbm.at[:, columns(theirs)], k_ref.at[1]),
                (v_hbm.at[:, columns(theirs)], v_ref.at[1]),
                (q_hbm.at[:, columns(theirs)], q_ref.at[1]),
                (g_hbm.at[:, columns(theirs)], g_ref.at[1]),
            )
        )
    ]
    outs = [
        to_partner(src, dst.at[:, columns(mine)], out_send.at[i], out_recv.at[i])
        for i, (src, dst) in enumerate(
            ((normed_out, normed_ref), (gq_out, gq_ref), (gk_out, gk_acc), (gv_out, gv_acc))
        )
    ]

    def close_copy(j, slot):
        return to_partner(bshare_out.at[j], back_in.at[slot], core_send.at[j], core_recv.at[j])

    def chip_copy(phase, src, dst, at_src, at_dst, other):
        return pltpu.make_async_remote_copy(
            src_ref=src.at[at_src],
            dst_ref=dst.at[at_dst],
            send_sem=chip_send.at[phase],
            recv_sem=chip_recv.at[phase],
            device_id=(2 * other + core, col),
            device_id_type=MESH,
        )

    def chip_start(phase, src, dst):
        for other in others:
            chip_copy(phase, src, dst, other, chip, other).start()

    every = pl.ds(0, chips - 1)

    def chip_wait(phase, src, dst):
        chip_copy(phase, src, dst, every, every, others[0]).wait_recv()

    def chip_sent(phase, src, dst):
        chip_copy(phase, src, dst, every, every, others[0]).wait_send()

    def put(ref, j, state):
        ref[pl.ds(j * pieces, pieces)] = state.astype(bf16).reshape(pieces, piece, HD)

    def take(ref, j):
        return ref[pl.ds(j * pieces, pieces)].reshape(HD, HD).astype(f32)

    @pl.when(core == 1)
    def _():
        pl.semaphore_wait(barrier, 1)
        pl.semaphore_signal(here, inc=1, device_id=(partner, col), device_id_type=MESH)

    @pl.when(core == 0)
    def _():
        pl.semaphore_wait(here, 1)

    for copy in ins:
        copy.start()
    for load in loads[2:]:
        load.start()

    def edges(ids):
        docs = ids.astype(f32)
        return (
            docs,
            jnp.where(docs == docs[:, :1], 1.0, 0.0).astype(bf16),
            jnp.where(docs == docs[:, tokens - 1 :], 1.0, 0.0).astype(bf16),
        )

    def tails(role, last_row):
        for j in range(half):
            at = lanes(j)
            pair[block[role], j] = dot(k_ref[role, :, at].T * last_row, v_ref[role, :, at], NN)

    marks = [edges(doc_ref[...]), None]
    loads[0].wait()
    loads[1].wait()
    tails(0, marks[0][2])
    for copy in ins[:3]:
        copy.wait_recv()
    marks[1] = edges(doc_in[...])
    tails(1, marks[1][2])

    both = flag(sg_ref[c2] <= c0)
    for j in range(half):
        put(sum_out, j, pair[1, j] + both * pair[0, j])
    sum_in[chip] = sum_out[chip]

    @pl.when(core == 0)
    def _():
        pl.semaphore_wait(barrier, 2 * (chips - 1) + 2 * (spread - 1))
        pl.semaphore_signal(go, inc=1, device_id=(partner, col), device_id_type=MESH)

    @pl.when(core == 1)
    def _():
        pl.semaphore_wait(go, 1)

    chip_start(0, sum_out, sum_in)

    causal = lax.broadcasted_iota(jnp.int32, (tokens, tokens), 0) >= lax.broadcasted_iota(
        jnp.int32, (tokens, tokens), 1
    )
    for role in range(2):
        doc_row = jnp.broadcast_to(marks[role][0], (tokens, tokens))
        doc_col = doc_row.T
        same_ref[role] = jnp.where(causal & (doc_row == doc_col), 1.0, 0.0)
        own = doc_col[:, :HD]
        first_ref[role] = jnp.where(own == own[:1], 1.0, 0.0).astype(bf16)
        if role == 0:
            last_ref[...] = jnp.where(own == own[tokens - 1 :], 1.0, 0.0).astype(bf16)
    for load in loads[2:]:
        load.wait()
    for copy in ins[3:]:
        copy.wait_recv()

    for role in range(2):

        def local_forward(j, _, role=role):
            at = lanes(j)
            query = q_ref[role, :, at]
            scores = dot(query, k_ref[role, :, at], NT)
            weights = jnp.where(same_ref[role] > 0.5, scores, 0.0).astype(bf16)
            weights_ref[role, j] = weights
            att_ref[role, :, at] = dot(weights, v_ref[role, :, at], NN)
            qf_ref[role, :, at] = query * first_ref[role]
            qt_ref[role, j] = query.T * marks[role][1]
            scaled_ref[role, :, at] = gain_ref[:, lanes(mine + j)] * g_ref[role, :, at].astype(f32)
            if role == 0:
                kl_ref[:, lanes(mine + j)] = k_ref[0, :, at] * last_ref[...]
                vl_ref[:, lanes(mine + j)] = v_ref[0, :, at] * last_ref[...]
                kl_ref[:, lanes(theirs + j)] = kx_ref[:, at] * last_ref[...]
                vl_ref[:, lanes(theirs + j)] = vx_ref[:, at] * last_ref[...]
            return _

        lax.fori_loop(0, half, local_forward, 0)

    chip_wait(0, sum_out, sum_in)
    run = jnp.zeros((piece, HD), f32)
    run_out[0] = run.astype(bf16)
    for w in range(1, chips):
        begin = sg_ref[2 * w]
        run = flag(begin <= 2 * w - 1) * (sum_in[w - 1].astype(f32) + flag(begin < 2 * w - 2) * run)
        run_out[w] = run.astype(bf16)
    run_in[chip] = run_out[chip]
    chip_start(1, run_out, run_in)
    chip_wait(1, run_out, run_in)

    odd = core == 1
    inside, through = flag(sg_ref[c1] <= c0), flag(sg_ref[c1] < c0)
    own_a, own_b = jnp.where(odd, inside, 0.0), jnp.where(odd, through, 1.0)
    their_a, their_b = jnp.where(odd, 0.0, inside), jnp.where(odd, 1.0, through)
    for j in range(half):
        state, entering = pair[0, j], take(run_in, j)
        carry_ref[0, j] = (own_a * state + own_b * entering).astype(bf16)
        carry_ref[1, j] = (their_a * state + their_b * entering).astype(bf16)

    for role in range(2):
        square = jnp.zeros((tokens, HD), f32)
        cross = jnp.zeros((tokens, HD), f32)
        for j in range(half):
            at = lanes(j)
            att = att_ref[role, :, at] + dot(qf_ref[role, :, at], carry_ref[role, j], NN)
            att_ref[role, :, at] = att
            square = square + att * att
            cross = cross + scaled_ref[role, :, at] * att
        rows_out[block[role], 0:1] = jnp.sum(square.T, axis=0, keepdims=True)
        rows_out[block[role], 1:2] = jnp.sum(cross.T, axis=0, keepdims=True)

    own_slot = 2 * col + core

    def x_copy(slot, peer):
        return pltpu.make_async_remote_copy(
            src_ref=rows_out,
            dst_ref=rows_in.at[slot],
            send_sem=x_send.at[peer],
            recv_sem=x_recv.at[slot],
            device_id=(c0 + lax.rem(peer, 2), lax.div(peer, 2)),
            device_id_type=MESH,
        )

    peers = [
        2 * lax.rem(col + d, spread) + lax.rem(core + e, 2)
        for d in sorted(range(spread), key=lambda d: -hops(d, spread))
        for e in range(2)
        if d or e
    ]
    for peer in peers:
        x_copy(own_slot, peer).start()
    sums = rows_out[...]
    for peer in reversed(peers):
        x_copy(peer, peer).wait_recv()
        sums = sums + rows_in[peer]
    rows_out_sum = sums
    inverse = lax.rsqrt(rows_out_sum[:, 0:1] / width + EPSILON)
    coef = inverse * inverse * inverse * rows_out_sum[:, 1:2] / width
    for b in range(2):
        at_role = jnp.where(core == b, 0, 1)
        inv_ref[at_role] = jnp.broadcast_to(inverse[b], (HD, tokens)).T
        coef_ref[at_role] = jnp.broadcast_to(coef[b], (HD, tokens)).T

    for role in range(2):
        for j in range(half):
            at = lanes(j)
            ga = inv_ref[role] * scaled_ref[role, :, at] - coef_ref[role] * att_ref[role, :, at]
            ga = ga.astype(bf16)
            ga_ref[role, :, at] = ga
            bpair[block[role], j] = dot(qt_ref[role, j], ga, NN)

    from_first, from_second = flag(sg_ref[c0] < c0), flag(sg_ref[c1] < c0)
    for j in range(half):
        put(bsum_out, j, from_first * bpair[0, j] + from_second * bpair[1, j])
    bsum_in[chip] = bsum_out[chip]
    chip_start(2, bsum_out, bsum_in)

    def local_backward(role, to_normed, to_gq, to_gk, to_gv, first):
        def one(j, _):
            at = lanes(j)
            to = lanes(first + j)
            ga = ga_ref[role, :, at]
            normed = att_ref[role, :, at] * inv_ref[role] * gain_ref[:, lanes(mine + j)]
            to_normed[:, to] = normed.astype(bf16)
            scores = dot(ga, v_ref[role, :, at], NT)
            scores = jnp.where(same_ref[role] > 0.5, scores, 0.0).astype(bf16)
            part = dot(ga * first_ref[role], carry_ref[role, j], NT)
            to_gq[:, to] = (dot(scores, k_ref[role, :, at], NN) + part).astype(bf16)
            to_gk[:, to] = dot(scores, q_ref[role, :, at], TN)
            to_gv[:, to] = dot(weights_ref[role, j], ga, TN)
            return _

        lax.fori_loop(0, half, one, 0)

    local_backward(1, normed_out, gq_out, gk_out, gv_out, 0)
    for copy in outs:
        copy.start()

    chip_wait(2, bsum_out, bsum_in)
    run = jnp.zeros((piece, HD), f32)
    brun_out[chips - 1] = run.astype(bf16)
    for w in range(chips - 2, -1, -1):
        run = flag(sg_ref[min(2 * w + 4, groups - 1)] <= 2 * w + 1) * run
        run = flag(sg_ref[2 * w + 2] <= 2 * w + 1) * (bsum_in[w + 1].astype(f32) + run)
        brun_out[w] = run.astype(bf16)
    brun_in[chip] = brun_out[chip]
    chip_start(3, brun_out, brun_in)

    local_backward(0, normed_ref, gq_ref, gk_acc, gv_acc, mine)

    chip_wait(3, brun_out, brun_in)
    reach = flag(sg_ref[c2] <= c0)
    own_a, own_b = jnp.where(odd, 0.0, inside), jnp.where(odd, 1.0, reach)
    their_a, their_b = jnp.where(odd, inside, 0.0), jnp.where(odd, reach, 1.0)
    for j in range(half):
        bshare_out[j] = (their_a * bpair[1, j] + their_b * take(brun_in, j)).astype(bf16)
        close_copy(j, mine + j).start()
    for j in range(half):
        back_in[mine + j] = (own_a * bpair[1, j] + own_b * take(brun_in, j)).astype(bf16)

    for j in range(half):
        close_copy(j, theirs + j).wait_recv()

    for phase, src, dst in ((0, sum_out, sum_in), (1, run_out, run_in), (2, bsum_out, bsum_in), (3, brun_out, brun_in)):
        chip_sent(phase, src, dst)
    for copy in ins:
        copy.wait_send()
    for copy in outs:
        copy.wait_send()
        copy.wait_recv()
    for j in range(half):
        close_copy(j, mine + j).wait_send()
    for peer in peers:
        x_copy(own_slot, peer).wait_send()


def finish(
    normed_ref, gq_ref, gk_acc, gv_acc, kl_ref, vl_ref, back_ref,
    normed_out, gq_out, gk_out, gv_out,
    gk_ref, gv_ref, sem,
):
    heads = back_ref.shape[0]
    copies = [
        pltpu.make_async_copy(normed_ref, normed_out, sem.at[0]),
        pltpu.make_async_copy(gq_ref, gq_out, sem.at[1]),
    ]
    for copy in copies:
        copy.start()
    for h in range(heads):
        at = slice(h * HD, (h + 1) * HD)
        gk_ref[:, at] = (gk_acc[:, at] + dot(vl_ref[:, at], back_ref[h], NT)).astype(bf16)
        gv_ref[:, at] = (gv_acc[:, at] + dot(kl_ref[:, at], back_ref[h], NN)).astype(bf16)
        if h % 2 == 1:
            done = pl.ds((h - 1) * HD, 2 * HD)
            for i, (src, dst) in enumerate(((gk_ref, gk_out), (gv_ref, gv_out))):
                copy = pltpu.make_async_copy(src.at[:, done], dst.at[:, done], sem.at[h + 1 + i])
                copy.start()
                copies.append(copy)
    for copy in copies:
        copy.wait()


def solution(mesh):
    groups, spread = mesh.shape["seq"], mesh.shape["head"]
    chips = groups // 2
    ring = 4 if chips % 4 == 0 else 1

    def local(query_in, key_in, value_in, out_grad, norm_gain, doc_ids, start_group):
        tokens, columns = query_in.shape
        heads = columns // HD
        half = heads // 2
        vmem = pl.BlockSpec(memory_space=pltpu.VMEM)
        hbm = pl.BlockSpec(memory_space=pltpu.HBM)
        pair = pltpu.VMEM((2, half, HD, HD), f32)
        pieces = pltpu.VMEM((chips, half * HD // chips, HD), bf16)
        closed = pltpu.VMEM((half, HD, HD), bf16)
        narrow = pltpu.VMEM((2, tokens, HD), bf16)
        row = pltpu.VMEM((2, tokens, HD), f32)
        wide_b = pltpu.VMEM((tokens, columns), bf16)
        wide_f = pltpu.VMEM((tokens, columns), f32)
        half_b = pltpu.VMEM((tokens, columns // 2), bf16)
        half_f = pltpu.VMEM((tokens, columns // 2), f32)
        both_b = pltpu.VMEM((2, tokens, columns // 2), bf16)
        both_f = pltpu.VMEM((2, tokens, columns // 2), f32)
        dma = pltpu.SemaphoreType.DMA
        outs = pl.pallas_call(
            functools.partial(kernel, chips, ring, heads, spread, columns * spread),
            out_shape=[wide_b, wide_b, wide_f, wide_f, wide_b, wide_b, pltpu.VMEM((heads, HD, HD), bf16)],
            in_specs=[pl.BlockSpec(memory_space=pltpu.SMEM), vmem] + [hbm] * 4 + [vmem],
            out_specs=[vmem] * 7,
            scratch_shapes=[
                *[both_b] * 4,
                pltpu.VMEM((1, tokens), jnp.int32),
                half_b,
                half_b,
                pltpu.VMEM((2, tokens, tokens), f32),
                narrow,
                pltpu.VMEM((tokens, HD), bf16),
                row,
                row,
                pltpu.VMEM((2, half, tokens, tokens), bf16),
                both_f,
                both_b,
                both_b,
                pltpu.VMEM((2, half, HD, tokens), bf16),
                both_f,
                *[pair, pieces, pieces, pieces, pieces],
                pltpu.VMEM((2, half, HD, HD), bf16),
                *[pair, pieces, pieces, pieces, pieces],
                closed,
                pltpu.VMEM((2, 2, tokens), f32),
                pltpu.VMEM((2 * spread, 2, 2, tokens), f32),
                half_b,
                half_b,
                half_f,
                half_f,
                dma((6,)),
                dma((4,)),
                dma((4,)),
                dma((5,)),
                dma((5,)),
                dma((4,)),
                dma((4,)),
                dma((half,)),
                dma((half,)),
                dma((2 * spread,)),
                dma((2 * spread,)),
                pltpu.SemaphoreType.REGULAR,
                pltpu.SemaphoreType.REGULAR,
            ],
            compiler_params=pltpu.CompilerParams(
                collective_id=0, has_side_effects=True, vmem_limit_bytes=62_300_000
            ),
            name="attention",
        )(
            start_group,
            doc_ids.reshape(1, tokens),
            query_in,
            key_in,
            value_in,
            out_grad,
            norm_gain.reshape(1, columns),
        )
        return pl.pallas_call(
            finish,
            out_shape=[jax.ShapeDtypeStruct((tokens, columns), bf16)] * 4,
            in_specs=[vmem] * 7,
            out_specs=[pl.BlockSpec(memory_space=pl.ANY)] * 4,
            scratch_shapes=[wide_b, wide_b, pltpu.SemaphoreType.DMA((heads + 2,))],
            compiler_params=pltpu.CompilerParams(vmem_limit_bytes=4 << 20),
            name="finish",
        )(*outs)

    wide = P("seq", "head")
    return jax.shard_map(
        local,
        mesh=mesh,
        in_specs=(wide, wide, wide, wide, P("head"), P("seq"), P()),
        out_specs=(wide, wide, wide, wide),
        check_vma=False,
    )
```

```python
import functools

import jax
import jax.numpy as jnp
from jax import lax
from jax.experimental import pallas as pl
from jax.experimental.pallas import tpu as pltpu
from jax.sharding import PartitionSpec as P

HD = 128
EPSILON = 1e-06
MESH = pl.DeviceIdType.MESH
f32, bf16 = jnp.float32, jnp.bfloat16


def dot(a, b, contract):
    return lax.dot_general(a, b, (contract, ((), ())), preferred_element_type=f32)


NN = ((1,), (0,))
NT = ((1,), (1,))
TN = ((0,), (0,))


def kernel(
    chips, ring, heads, spread, width,
    sg_hbm, doc_hbm, q_hbm, k_hbm, v_hbm, g_hbm, gain_hbm,
    normed_ref, gq_ref, gk_acc, gv_acc, kl_ref, vl_ref, back_in,
    sg_ref, doc_ref, gain_ref, q_ref, k_ref, v_ref, g_ref, doc_in, kx_ref, vx_ref,
    same_ref, first_ref, last_ref, inv_ref, coef_ref,
    weights_ref, att_ref, ga_ref, qf_ref, qt_ref, scaled_ref,
    pair, sum_out, sum_in, run_out, run_in, carry_ref,
    bpair, bsum_out, bsum_in, brun_out, brun_in, bshare_out,
    rows_out, rows_in, normed_out, gq_out, gk_out, gv_out,
    load_sem, chip_send, chip_recv, in_send, in_recv, out_send, out_recv, core_send, core_recv,
    x_send, x_recv, here, go,
):
    seq, col = lax.axis_index("seq"), lax.axis_index("head")
    chip, core = lax.div(seq, 2), lax.rem(seq, 2)
    partner = seq + 1 - 2 * core
    tokens = q_ref.shape[1]
    half = heads // 2
    piece = sum_out.shape[1]
    pieces = HD // piece
    mine, theirs = core * half, (1 - core) * half
    c0, c1, groups = 2 * chip, 2 * chip + 1, 2 * chips
    c2 = jnp.minimum(c0 + 2, groups - 1)
    lines = chips // ring
    block = (core, 1 - core)

    def columns(first):
        return pl.ds(pl.multiple_of(first * HD, HD), half * HD)

    loads = [
        pltpu.make_async_copy(src.at[:, columns(first)], dst, load_sem.at[i])
        for i, (src, first, dst) in enumerate(
            (
                (k_hbm, mine, k_ref.at[0]),
                (v_hbm, mine, v_ref.at[0]),
                (q_hbm, mine, q_ref.at[0]),
                (g_hbm, mine, g_ref.at[0]),
                (k_hbm, theirs, kx_ref),
                (v_hbm, theirs, vx_ref),
            )
        )
    ]
    smalls = [
        pltpu.make_async_copy(src, dst, load_sem.at[len(loads) + i])
        for i, (src, dst) in enumerate(((doc_hbm, doc_ref), (sg_hbm, sg_ref), (gain_hbm, gain_ref)))
    ]

    def hops(offset, size):
        return min(offset, size - offset)

    offsets = sorted(
        ((dz, dy) for dz in range(lines) for dy in range(ring) if dz or dy),
        key=lambda o: -(hops(o[0], lines) + hops(o[1], ring)),
    )
    chip_z, chip_y = lax.div(chip, ring), lax.rem(chip, ring)
    others = [lax.rem(chip_z + dz, lines) * ring + lax.rem(chip_y + dy, ring) for dz, dy in offsets]

    barrier = pltpu.get_barrier_semaphore()

    @pl.when(core == 0)
    def _():
        pl.semaphore_signal(barrier, inc=1, device_id=(partner, col), device_id_type=MESH)

    for other in others:
        pl.semaphore_signal(barrier, inc=1, device_id=(2 * other, col), device_id_type=MESH)
    for d in range(1, spread):
        pl.semaphore_signal(barrier, inc=1, device_id=(c0, lax.rem(col + d, spread)), device_id_type=MESH)

    for copy in smalls[:2] + loads[:2] + smalls[2:]:
        copy.start()

    def lanes(h):
        return pl.ds(pl.multiple_of(h * HD, HD), HD)

    def flag(condition):
        return jnp.where(condition, 1.0, 0.0).astype(f32)

    def to_partner(src, dst, send, recv):
        return pltpu.make_async_remote_copy(
            src_ref=src, dst_ref=dst, send_sem=send, recv_sem=recv, device_id=(partner, col), device_id_type=MESH
        )

    ins = [
        to_partner(src, dst, in_send.at[i], in_recv.at[i])
        for i, (src, dst) in enumerate(
            (
                (doc_hbm, doc_in),
                (k_hbm.at[:, columns(theirs)], k_ref.at[1]),
                (v_hbm.at[:, columns(theirs)], v_ref.at[1]),
                (q_hbm.at[:, columns(theirs)], q_ref.at[1]),
                (g_hbm.at[:, columns(theirs)], g_ref.at[1]),
            )
        )
    ]
    outs = [
        to_partner(src, dst.at[:, columns(mine)], out_send.at[i], out_recv.at[i])
        for i, (src, dst) in enumerate(
            ((normed_out, normed_ref), (gq_out, gq_ref), (gk_out, gk_acc), (gv_out, gv_acc))
        )
    ]

    def close_copy(j, slot):
        return to_partner(bshare_out.at[j], back_in.at[slot], core_send.at[j], core_recv.at[j])

    def chip_copy(phase, src, dst, at_src, at_dst, other):
        return pltpu.make_async_remote_copy(
            src_ref=src.at[at_src],
            dst_ref=dst.at[at_dst],
            send_sem=chip_send.at[phase],
            recv_sem=chip_recv.at[phase],
            device_id=(2 * other + core, col),
            device_id_type=MESH,
        )

    def chip_start(phase, src, dst):
        for other in others:
            chip_copy(phase, src, dst, other, chip, other).start()

    every = pl.ds(0, chips - 1)

    def chip_wait(phase, src, dst):
        chip_copy(phase, src, dst, every, every, others[0]).wait_recv()

    def chip_sent(phase, src, dst):
        chip_copy(phase, src, dst, every, every, others[0]).wait_send()

    def put(ref, j, state):
        ref[pl.ds(j * pieces, pieces)] = state.astype(bf16).reshape(pieces, piece, HD)

    def take(ref, j):
        return ref[pl.ds(j * pieces, pieces)].reshape(HD, HD).astype(f32)

    @pl.when(core == 1)
    def _():
        pl.semaphore_wait(barrier, 1)
        pl.semaphore_signal(here, inc=1, device_id=(partner, col), device_id_type=MESH)

    @pl.when(core == 0)
    def _():
        pl.semaphore_wait(here, 1)

    for copy in ins:
        copy.start()
    for load in loads[2:]:
        load.start()

    def edges(ids):
        docs = ids.astype(f32)
        return (
            docs,
            jnp.where(docs == docs[:, :1], 1.0, 0.0).astype(bf16),
            jnp.where(docs == docs[:, tokens - 1 :], 1.0, 0.0).astype(bf16),
        )

    def tails(role, last_row):
        for j in range(half):
            at = lanes(j)
            pair[block[role], j] = dot(k_ref[role, :, at].T * last_row, v_ref[role, :, at], NN)

    smalls[0].wait()
    marks = [edges(doc_ref[...]), None]
    loads[0].wait()
    loads[1].wait()
    tails(0, marks[0][2])
    for copy in ins[:3]:
        copy.wait_recv()
    marks[1] = edges(doc_in[...])
    tails(1, marks[1][2])

    smalls[1].wait()
    both = flag(sg_ref[c2] <= c0)
    for j in range(half):
        put(sum_out, j, pair[1, j] + both * pair[0, j])
    sum_in[chip] = sum_out[chip]

    @pl.when(core == 0)
    def _():
        pl.semaphore_wait(barrier, 2 * (chips - 1) + 2 * (spread - 1))
        pl.semaphore_signal(go, inc=1, device_id=(partner, col), device_id_type=MESH)

    @pl.when(core == 1)
    def _():
        pl.semaphore_wait(go, 1)

    chip_start(0, sum_out, sum_in)

    causal = lax.broadcasted_iota(jnp.int32, (tokens, tokens), 0) >= lax.broadcasted_iota(
        jnp.int32, (tokens, tokens), 1
    )
    for role in range(2):
        doc_row = jnp.broadcast_to(marks[role][0], (tokens, tokens))
        doc_col = doc_row.T
        same_ref[role] = jnp.where(causal & (doc_row == doc_col), 1.0, 0.0)
        own = doc_col[:, :HD]
        first_ref[role] = jnp.where(own == own[:1], 1.0, 0.0).astype(bf16)
        if role == 0:
            last_ref[...] = jnp.where(own == own[tokens - 1 :], 1.0, 0.0).astype(bf16)
    smalls[2].wait()
    for load in loads[2:]:
        load.wait()
    for copy in ins[3:]:
        copy.wait_recv()

    for role in range(2):

        def local_forward(j, _, role=role):
            at = lanes(j)
            query = q_ref[role, :, at]
            scores = dot(query, k_ref[role, :, at], NT)
            weights = jnp.where(same_ref[role] > 0.5, scores, 0.0).astype(bf16)
            weights_ref[role, j] = weights
            att_ref[role, :, at] = dot(weights, v_ref[role, :, at], NN)
            qf_ref[role, :, at] = query * first_ref[role]
            qt_ref[role, j] = query.T * marks[role][1]
            scaled_ref[role, :, at] = gain_ref[:, lanes(mine + j)] * g_ref[role, :, at].astype(f32)
            if role == 0:
                kl_ref[:, lanes(mine + j)] = k_ref[0, :, at] * last_ref[...]
                vl_ref[:, lanes(mine + j)] = v_ref[0, :, at] * last_ref[...]
                kl_ref[:, lanes(theirs + j)] = kx_ref[:, at] * last_ref[...]
                vl_ref[:, lanes(theirs + j)] = vx_ref[:, at] * last_ref[...]
            return _

        lax.fori_loop(0, half, local_forward, 0)

    chip_wait(0, sum_out, sum_in)
    inner = [[jnp.zeros((piece, HD), f32)] for _ in range(lines)]
    for i in range(1, ring + 1):
        for line in range(lines):
            w = line * ring + i
            if w < chips:
                begin = sg_ref[2 * w]
                value = sum_in[w - 1].astype(f32)
                if i > 1:
                    value = value + flag(begin < 2 * w - 2) * inner[line][-1]
                inner[line].append(flag(begin <= 2 * w - 1) * value)
    run = None
    for line in range(lines):
        for i in range(ring):
            w = line * ring + i
            value = inner[line][i]
            if line > 0:
                value = value + flag(sg_ref[2 * w] < 2 * line * ring) * run
            run_out[w] = value.astype(bf16)
        if line + 1 < lines:
            value = inner[line][ring]
            if line > 0:
                value = value + flag(sg_ref[2 * (line + 1) * ring] < 2 * line * ring) * run
            run = value
    run_in[chip] = run_out[chip]
    chip_start(1, run_out, run_in)
    chip_wait(1, run_out, run_in)

    odd = core == 1
    inside, through = flag(sg_ref[c1] <= c0), flag(sg_ref[c1] < c0)
    own_a, own_b = jnp.where(odd, inside, 0.0), jnp.where(odd, through, 1.0)
    their_a, their_b = jnp.where(odd, 0.0, inside), jnp.where(odd, 1.0, through)
    for j in range(half):
        state, entering = pair[0, j], take(run_in, j)
        carry_ref[0, j] = (own_a * state + own_b * entering).astype(bf16)
        carry_ref[1, j] = (their_a * state + their_b * entering).astype(bf16)

    for role in range(2):
        square = jnp.zeros((tokens, HD), f32)
        cross = jnp.zeros((tokens, HD), f32)
        for j in range(half):
            at = lanes(j)
            att = att_ref[role, :, at] + dot(qf_ref[role, :, at], carry_ref[role, j], NN)
            att_ref[role, :, at] = att
            square = square + att * att
            cross = cross + scaled_ref[role, :, at] * att
        rows_out[block[role], 0:1] = jnp.sum(square.T, axis=0, keepdims=True)
        rows_out[block[role], 1:2] = jnp.sum(cross.T, axis=0, keepdims=True)

    own_slot = 2 * col + core

    def x_copy(slot, peer):
        return pltpu.make_async_remote_copy(
            src_ref=rows_out,
            dst_ref=rows_in.at[slot],
            send_sem=x_send.at[peer],
            recv_sem=x_recv.at[slot],
            device_id=(c0 + lax.rem(peer, 2), lax.div(peer, 2)),
            device_id_type=MESH,
        )

    peers = [
        2 * lax.rem(col + d, spread) + lax.rem(core + e, 2)
        for d in sorted(range(spread), key=lambda d: -hops(d, spread))
        for e in range(2)
        if d or e
    ]
    for peer in peers:
        x_copy(own_slot, peer).start()
    sums = rows_out[...]
    for peer in reversed(peers):
        x_copy(peer, peer).wait_recv()
        sums = sums + rows_in[peer]
    rows_out_sum = sums
    inverse = lax.rsqrt(rows_out_sum[:, 0:1] / width + EPSILON)
    coef = inverse * inverse * inverse * rows_out_sum[:, 1:2] / width
    for b in range(2):
        at_role = jnp.where(core == b, 0, 1)
        inv_ref[at_role] = jnp.broadcast_to(inverse[b], (HD, tokens)).T
        coef_ref[at_role] = jnp.broadcast_to(coef[b], (HD, tokens)).T

    for role in range(2):
        for j in range(half):
            at = lanes(j)
            ga = inv_ref[role] * scaled_ref[role, :, at] - coef_ref[role] * att_ref[role, :, at]
            ga = ga.astype(bf16)
            ga_ref[role, :, at] = ga
            bpair[block[role], j] = dot(qt_ref[role, j], ga, NN)

    from_first, from_second = flag(sg_ref[c0] < c0), flag(sg_ref[c1] < c0)
    for j in range(half):
        put(bsum_out, j, from_first * bpair[0, j] + from_second * bpair[1, j])
    bsum_in[chip] = bsum_out[chip]
    chip_start(2, bsum_out, bsum_in)

    def local_backward(role, to_normed, to_gq, to_gk, to_gv, first):
        def one(j, _):
            at = lanes(j)
            to = lanes(first + j)
            ga = ga_ref[role, :, at]
            normed = att_ref[role, :, at] * inv_ref[role] * gain_ref[:, lanes(mine + j)]
            to_normed[:, to] = normed.astype(bf16)
            scores = dot(ga, v_ref[role, :, at], NT)
            scores = jnp.where(same_ref[role] > 0.5, scores, 0.0).astype(bf16)
            part = dot(ga * first_ref[role], carry_ref[role, j], NT)
            to_gq[:, to] = (dot(scores, k_ref[role, :, at], NN) + part).astype(bf16)
            to_gk[:, to] = dot(scores, q_ref[role, :, at], TN)
            to_gv[:, to] = dot(weights_ref[role, j], ga, TN)
            return _

        lax.fori_loop(0, half, one, 0)

    local_backward(1, normed_out, gq_out, gk_out, gv_out, 0)
    for copy in outs:
        copy.start()

    chip_wait(2, bsum_out, bsum_in)
    inner = [[None] * ring for _ in range(lines)]
    for i in range(ring - 1, -1, -1):
        for line in range(lines):
            w = line * ring + i
            if i == ring - 1:
                inner[line][i] = jnp.zeros((piece, HD), f32)
            else:
                value = bsum_in[w + 1].astype(f32)
                if i < ring - 2:
                    value = value + flag(sg_ref[2 * w + 4] <= 2 * w + 1) * inner[line][i + 1]
                inner[line][i] = flag(sg_ref[2 * w + 2] <= 2 * w + 1) * value
    run = None
    for line in range(lines - 1, -1, -1):
        behind = (line + 1) * ring
        for i in range(ring - 1, -1, -1):
            w = line * ring + i
            value = inner[line][i]
            if line + 1 < lines:
                value = value + flag(sg_ref[2 * behind] <= 2 * w + 1) * run
            brun_out[w] = value.astype(bf16)
        if line > 0:
            w = line * ring
            value = bsum_in[w].astype(f32) + flag(sg_ref[2 * w + 2] <= 2 * w - 1) * inner[line][0]
            if line + 1 < lines:
                value = value + flag(sg_ref[2 * behind] <= 2 * w - 1) * run
            run = value
    brun_in[chip] = brun_out[chip]
    chip_start(3, brun_out, brun_in)

    local_backward(0, normed_ref, gq_ref, gk_acc, gv_acc, mine)

    chip_wait(3, brun_out, brun_in)
    reach = flag(sg_ref[c2] <= c0)
    own_a, own_b = jnp.where(odd, 0.0, inside), jnp.where(odd, 1.0, reach)
    their_a, their_b = jnp.where(odd, inside, 0.0), jnp.where(odd, reach, 1.0)
    for j in range(half):
        bshare_out[j] = (their_a * bpair[1, j] + their_b * take(brun_in, j)).astype(bf16)
        close_copy(j, mine + j).start()
    for j in range(half):
        back_in[mine + j] = (own_a * bpair[1, j] + own_b * take(brun_in, j)).astype(bf16)

    for j in range(half):
        close_copy(j, theirs + j).wait_recv()

    for phase, src, dst in ((0, sum_out, sum_in), (1, run_out, run_in), (2, bsum_out, bsum_in), (3, brun_out, brun_in)):
        chip_sent(phase, src, dst)
    for copy in ins:
        copy.wait_send()
    for copy in outs:
        copy.wait_send()
        copy.wait_recv()
    for j in range(half):
        close_copy(j, mine + j).wait_send()
    for peer in peers:
        x_copy(own_slot, peer).wait_send()


def finish(
    normed_ref, gq_ref, gk_acc, gv_acc, kl_ref, vl_ref, back_ref,
    normed_out, gq_out, gk_out, gv_out,
    gk_ref, gv_ref, sem,
):
    heads = back_ref.shape[0]
    copies = [
        pltpu.make_async_copy(normed_ref, normed_out, sem.at[0]),
        pltpu.make_async_copy(gq_ref, gq_out, sem.at[1]),
    ]
    for copy in copies:
        copy.start()
    for h in range(heads):
        at = slice(h * HD, (h + 1) * HD)
        gk_ref[:, at] = (gk_acc[:, at] + dot(vl_ref[:, at], back_ref[h], NT)).astype(bf16)
        gv_ref[:, at] = (gv_acc[:, at] + dot(kl_ref[:, at], back_ref[h], NN)).astype(bf16)
        if h % 2 == 1:
            done = pl.ds((h - 1) * HD, 2 * HD)
            for i, (src, dst) in enumerate(((gk_ref, gk_out), (gv_ref, gv_out))):
                copy = pltpu.make_async_copy(src.at[:, done], dst.at[:, done], sem.at[h + 1 + i])
                copy.start()
                copies.append(copy)
    for copy in copies:
        copy.wait()


def solution(mesh):
    groups, spread = mesh.shape["seq"], mesh.shape["head"]
    chips = groups // 2
    ring = 4 if chips % 4 == 0 else 1

    def local(query_in, key_in, value_in, out_grad, norm_gain, doc_ids, start_group):
        tokens, columns = query_in.shape
        heads = columns // HD
        half = heads // 2
        vmem = pl.BlockSpec(memory_space=pltpu.VMEM)
        hbm = pl.BlockSpec(memory_space=pltpu.HBM)
        pair = pltpu.VMEM((2, half, HD, HD), f32)
        pieces = pltpu.VMEM((chips, half * HD // chips, HD), bf16)
        closed = pltpu.VMEM((half, HD, HD), bf16)
        narrow = pltpu.VMEM((2, tokens, HD), bf16)
        row = pltpu.VMEM((2, tokens, HD), f32)
        wide_b = pltpu.VMEM((tokens, columns), bf16)
        wide_f = pltpu.VMEM((tokens, columns), f32)
        half_b = pltpu.VMEM((tokens, columns // 2), bf16)
        half_f = pltpu.VMEM((tokens, columns // 2), f32)
        both_b = pltpu.VMEM((2, tokens, columns // 2), bf16)
        both_f = pltpu.VMEM((2, tokens, columns // 2), f32)
        dma = pltpu.SemaphoreType.DMA
        outs = pl.pallas_call(
            functools.partial(kernel, chips, ring, heads, spread, columns * spread),
            out_shape=[wide_b, wide_b, wide_f, wide_f, wide_b, wide_b, pltpu.VMEM((heads, HD, HD), bf16)],
            in_specs=[hbm] * 7,
            out_specs=[vmem] * 7,
            scratch_shapes=[
                pltpu.SMEM((groups,), jnp.int32),
                pltpu.VMEM((1, tokens), jnp.int32),
                pltpu.VMEM((1, columns), f32),
                *[both_b] * 4,
                pltpu.VMEM((1, tokens), jnp.int32),
                half_b,
                half_b,
                pltpu.VMEM((2, tokens, tokens), f32),
                narrow,
                pltpu.VMEM((tokens, HD), bf16),
                row,
                row,
                pltpu.VMEM((2, half, tokens, tokens), bf16),
                both_f,
                both_b,
                both_b,
                pltpu.VMEM((2, half, HD, tokens), bf16),
                both_f,
                *[pair, pieces, pieces, pieces, pieces],
                pltpu.VMEM((2, half, HD, HD), bf16),
                *[pair, pieces, pieces, pieces, pieces],
                closed,
                pltpu.VMEM((2, 2, tokens), f32),
                pltpu.VMEM((2 * spread, 2, 2, tokens), f32),
                half_b,
                half_b,
                half_f,
                half_f,
                dma((9,)),
                dma((4,)),
                dma((4,)),
                dma((5,)),
                dma((5,)),
                dma((4,)),
                dma((4,)),
                dma((half,)),
                dma((half,)),
                dma((2 * spread,)),
                dma((2 * spread,)),
                pltpu.SemaphoreType.REGULAR,
                pltpu.SemaphoreType.REGULAR,
            ],
            compiler_params=pltpu.CompilerParams(
                collective_id=0, has_side_effects=True, vmem_limit_bytes=62_300_000
            ),
            name="attention",
        )(
            start_group,
            doc_ids.reshape(1, tokens),
            query_in,
            key_in,
            value_in,
            out_grad,
            norm_gain.reshape(1, columns),
        )
        return pl.pallas_call(
            finish,
            out_shape=[jax.ShapeDtypeStruct((tokens, columns), bf16)] * 4,
            in_specs=[vmem] * 7,
            out_specs=[pl.BlockSpec(memory_space=pl.ANY)] * 4,
            scratch_shapes=[wide_b, wide_b, pltpu.SemaphoreType.DMA((heads + 2,))],
            compiler_params=pltpu.CompilerParams(vmem_limit_bytes=4 << 20),
            name="finish",
        )(*outs)

    wide = P("seq", "head")
    return jax.shard_map(
        local,
        mesh=mesh,
        in_specs=(wide, wide, wide, wide, P("head"), P("seq"), P()),
        out_specs=(wide, wide, wide, wide),
        check_vma=False,
    )
```

```python
import functools

import jax
import jax.numpy as jnp
from jax import lax
from jax.experimental import pallas as pl
from jax.experimental.pallas import tpu as pltpu
from jax.sharding import PartitionSpec as P

HD = 128
EPSILON = 1e-06
MESH = pl.DeviceIdType.MESH
f32, bf16 = jnp.float32, jnp.bfloat16


def dot(a, b, contract):
    return lax.dot_general(a, b, (contract, ((), ())), preferred_element_type=f32)


NN = ((1,), (0,))
NT = ((1,), (1,))
TN = ((0,), (0,))


def kernel(
    chips, ring, heads, spread, width,
    sg_hbm, doc_hbm, q_hbm, k_hbm, v_hbm, g_hbm, gain_hbm,
    normed_ref, gq_ref, gk_acc, gv_acc, kl_ref, vl_ref, back_in,
    sg_ref, doc_ref, gain_ref, q_ref, k_ref, v_ref, g_ref, doc_in, kx_ref, vx_ref,
    same_ref, first_ref, last_ref, inv_ref, coef_ref,
    weights_ref, att_ref, ga_ref, qf_ref, qt_ref, scaled_ref,
    pair, sum_out, sum_in, run_out, run_in, carry_ref,
    bpair, bsum_out, bsum_in, brun_out, brun_in, bshare_out,
    rows_out, rows_in, normed_out, gq_out, gk_out, gv_out,
    load_sem, chip_send, chip_recv, in_send, in_recv, out_send, out_recv, core_send, core_recv,
    x_send, x_recv, here, go,
):
    seq, col = lax.axis_index("seq"), lax.axis_index("head")
    chip, core = lax.div(seq, 2), lax.rem(seq, 2)
    partner = seq + 1 - 2 * core
    tokens = q_ref.shape[1]
    half = heads // 2
    piece = sum_out.shape[1]
    pieces = HD // piece
    mine, theirs = core * half, (1 - core) * half
    c0, c1, groups = 2 * chip, 2 * chip + 1, 2 * chips
    c2 = jnp.minimum(c0 + 2, groups - 1)
    lines = chips // ring
    block = (core, 1 - core)

    def columns(first):
        return pl.ds(pl.multiple_of(first * HD, HD), half * HD)

    loads = [
        pltpu.make_async_copy(src.at[:, columns(first)], dst, load_sem.at[i])
        for i, (src, first, dst) in enumerate(
            (
                (k_hbm, mine, k_ref.at[0]),
                (v_hbm, mine, v_ref.at[0]),
                (q_hbm, mine, q_ref.at[0]),
                (g_hbm, mine, g_ref.at[0]),
                (k_hbm, theirs, kx_ref),
                (v_hbm, theirs, vx_ref),
            )
        )
    ]
    smalls = [
        pltpu.make_async_copy(src, dst, load_sem.at[len(loads) + i])
        for i, (src, dst) in enumerate(((doc_hbm, doc_ref), (sg_hbm, sg_ref), (gain_hbm, gain_ref)))
    ]

    def hops(offset, size):
        return min(offset, size - offset)

    offsets = sorted(
        ((dz, dy) for dz in range(lines) for dy in range(ring) if dz or dy),
        key=lambda o: (-(hops(o[0], lines) + hops(o[1], ring)), -hops(o[1], ring), o),
    )
    chip_z, chip_y = lax.div(chip, ring), lax.rem(chip, ring)
    turn = 1 - 2 * core
    at_z = [lax.rem(chip_z + lines + turn * dz, lines) * ring for dz in range(lines)]
    at_y = [lax.rem(chip_y + ring + turn * dy, ring) for dy in range(ring)]
    others = [at_z[dz] + at_y[dy] for dz, dy in offsets]

    barrier = pltpu.get_barrier_semaphore()

    @pl.when(core == 0)
    def _():
        pl.semaphore_signal(barrier, inc=1, device_id=(partner, col), device_id_type=MESH)

    for other in others:
        pl.semaphore_signal(barrier, inc=1, device_id=(2 * other, col), device_id_type=MESH)
    for d in range(1, spread):
        pl.semaphore_signal(barrier, inc=1, device_id=(c0, lax.rem(col + d, spread)), device_id_type=MESH)

    for copy in smalls[:2] + loads[:2] + smalls[2:]:
        copy.start()

    def lanes(h):
        return pl.ds(pl.multiple_of(h * HD, HD), HD)

    def flag(condition):
        return jnp.where(condition, 1.0, 0.0).astype(f32)

    def to_partner(src, dst, send, recv):
        return pltpu.make_async_remote_copy(
            src_ref=src, dst_ref=dst, send_sem=send, recv_sem=recv, device_id=(partner, col), device_id_type=MESH
        )

    ins = [
        to_partner(src, dst, in_send.at[i], in_recv.at[i])
        for i, (src, dst) in enumerate(
            (
                (doc_hbm, doc_in),
                (k_hbm.at[:, columns(theirs)], k_ref.at[1]),
                (v_hbm.at[:, columns(theirs)], v_ref.at[1]),
                (q_hbm.at[:, columns(theirs)], q_ref.at[1]),
                (g_hbm.at[:, columns(theirs)], g_ref.at[1]),
            )
        )
    ]
    outs = [
        to_partner(src, dst.at[:, columns(mine)], out_send.at[i], out_recv.at[i])
        for i, (src, dst) in enumerate(
            ((normed_out, normed_ref), (gq_out, gq_ref), (gk_out, gk_acc), (gv_out, gv_acc))
        )
    ]

    def close_copy(j, slot):
        return to_partner(bshare_out.at[j], back_in.at[slot], core_send.at[j], core_recv.at[j])

    def chip_copy(phase, src, dst, at_src, at_dst, other):
        return pltpu.make_async_remote_copy(
            src_ref=src.at[at_src],
            dst_ref=dst.at[at_dst],
            send_sem=chip_send.at[phase],
            recv_sem=chip_recv.at[phase],
            device_id=(2 * other + core, col),
            device_id_type=MESH,
        )

    def chip_start(phase, src, dst):
        for other in others:
            chip_copy(phase, src, dst, other, chip, other).start()

    every = pl.ds(0, chips - 1)

    def chip_wait(phase, src, dst):
        chip_copy(phase, src, dst, every, every, others[0]).wait_recv()

    def chip_sent(phase, src, dst):
        chip_copy(phase, src, dst, every, every, others[0]).wait_send()

    def put(ref, j, state):
        ref[pl.ds(j * pieces, pieces)] = state.astype(bf16).reshape(pieces, piece, HD)

    def take(ref, j):
        return ref[pl.ds(j * pieces, pieces)].reshape(HD, HD).astype(f32)

    @pl.when(core == 1)
    def _():
        pl.semaphore_wait(barrier, 1)
        pl.semaphore_signal(here, inc=1, device_id=(partner, col), device_id_type=MESH)

    @pl.when(core == 0)
    def _():
        pl.semaphore_wait(here, 1)

    for copy in ins:
        copy.start()
    for load in loads[2:]:
        load.start()

    def edges(ids):
        docs = ids.astype(f32)
        return (
            docs,
            jnp.where(docs == docs[:, :1], 1.0, 0.0).astype(bf16),
            jnp.where(docs == docs[:, tokens - 1 :], 1.0, 0.0).astype(bf16),
        )

    def tails(role, last_row):
        for j in range(half):
            at = lanes(j)
            pair[block[role], j] = dot(k_ref[role, :, at].T * last_row, v_ref[role, :, at], NN)

    smalls[0].wait()
    marks = [edges(doc_ref[...]), None]
    loads[0].wait()
    loads[1].wait()
    tails(0, marks[0][2])
    for copy in ins[:3]:
        copy.wait_recv()
    marks[1] = edges(doc_in[...])
    tails(1, marks[1][2])

    smalls[1].wait()
    both = flag(sg_ref[c2] <= c0)
    for j in range(half):
        put(sum_out, j, pair[1, j] + both * pair[0, j])
    sum_in[chip] = sum_out[chip]

    @pl.when(core == 0)
    def _():
        pl.semaphore_wait(barrier, 2 * (chips - 1) + 2 * (spread - 1))
        pl.semaphore_signal(go, inc=1, device_id=(partner, col), device_id_type=MESH)

    @pl.when(core == 1)
    def _():
        pl.semaphore_wait(go, 1)

    chip_start(0, sum_out, sum_in)

    causal = lax.broadcasted_iota(jnp.int32, (tokens, tokens), 0) >= lax.broadcasted_iota(
        jnp.int32, (tokens, tokens), 1
    )
    for role in range(2):
        doc_row = jnp.broadcast_to(marks[role][0], (tokens, tokens))
        doc_col = doc_row.T
        same_ref[role] = jnp.where(causal & (doc_row == doc_col), 1.0, 0.0)
        own = doc_col[:, :HD]
        first_ref[role] = jnp.where(own == own[:1], 1.0, 0.0).astype(bf16)
        if role == 0:
            last_ref[...] = jnp.where(own == own[tokens - 1 :], 1.0, 0.0).astype(bf16)
    smalls[2].wait()
    for load in loads[2:]:
        load.wait()
    for copy in ins[3:]:
        copy.wait_recv()

    for role in range(2):

        def local_forward(j, _, role=role):
            at = lanes(j)
            query = q_ref[role, :, at]
            scores = dot(query, k_ref[role, :, at], NT)
            weights = jnp.where(same_ref[role] > 0.5, scores, 0.0).astype(bf16)
            weights_ref[role, j] = weights
            att_ref[role, :, at] = dot(weights, v_ref[role, :, at], NN)
            qf_ref[role, :, at] = query * first_ref[role]
            qt_ref[role, j] = query.T * marks[role][1]
            scaled_ref[role, :, at] = gain_ref[:, lanes(mine + j)] * g_ref[role, :, at].astype(f32)
            if role == 0:
                kl_ref[:, lanes(mine + j)] = k_ref[0, :, at] * last_ref[...]
                vl_ref[:, lanes(mine + j)] = v_ref[0, :, at] * last_ref[...]
                kl_ref[:, lanes(theirs + j)] = kx_ref[:, at] * last_ref[...]
                vl_ref[:, lanes(theirs + j)] = vx_ref[:, at] * last_ref[...]
            return _

        lax.fori_loop(0, half, local_forward, 0)

    chip_wait(0, sum_out, sum_in)
    inner = [[jnp.zeros((piece, HD), f32)] for _ in range(lines)]
    for i in range(1, ring + 1):
        for line in range(lines):
            w = line * ring + i
            if w < chips:
                begin = sg_ref[2 * w]
                value = sum_in[w - 1].astype(f32)
                if i > 1:
                    value = value + flag(begin < 2 * w - 2) * inner[line][-1]
                inner[line].append(flag(begin <= 2 * w - 1) * value)
    run = None
    for line in range(lines):
        for i in range(ring):
            w = line * ring + i
            value = inner[line][i]
            if line > 0:
                value = value + flag(sg_ref[2 * w] < 2 * line * ring) * run
            run_out[w] = value.astype(bf16)
        if line + 1 < lines:
            value = inner[line][ring]
            if line > 0:
                value = value + flag(sg_ref[2 * (line + 1) * ring] < 2 * line * ring) * run
            run = value
    run_in[chip] = run_out[chip]
    chip_start(1, run_out, run_in)
    chip_wait(1, run_out, run_in)

    odd = core == 1
    inside, through = flag(sg_ref[c1] <= c0), flag(sg_ref[c1] < c0)
    own_a, own_b = jnp.where(odd, inside, 0.0), jnp.where(odd, through, 1.0)
    their_a, their_b = jnp.where(odd, 0.0, inside), jnp.where(odd, 1.0, through)
    for j in range(half):
        state, entering = pair[0, j], take(run_in, j)
        carry_ref[0, j] = (own_a * state + own_b * entering).astype(bf16)
        carry_ref[1, j] = (their_a * state + their_b * entering).astype(bf16)

    for role in range(2):
        square = jnp.zeros((tokens, HD), f32)
        cross = jnp.zeros((tokens, HD), f32)
        for j in range(half):
            at = lanes(j)
            att = att_ref[role, :, at] + dot(qf_ref[role, :, at], carry_ref[role, j], NN)
            att_ref[role, :, at] = att
            square = square + att * att
            cross = cross + scaled_ref[role, :, at] * att
        rows_out[block[role], 0:1] = jnp.sum(square.T, axis=0, keepdims=True)
        rows_out[block[role], 1:2] = jnp.sum(cross.T, axis=0, keepdims=True)

    own_slot = 2 * col + core

    def x_copy(slot, peer):
        return pltpu.make_async_remote_copy(
            src_ref=rows_out,
            dst_ref=rows_in.at[slot],
            send_sem=x_send.at[peer],
            recv_sem=x_recv.at[slot],
            device_id=(c0 + lax.rem(peer, 2), lax.div(peer, 2)),
            device_id_type=MESH,
        )

    peers = [
        2 * lax.rem(col + d, spread) + lax.rem(core + e, 2)
        for d in sorted(range(spread), key=lambda d: -hops(d, spread))
        for e in range(2)
        if d or e
    ]
    for peer in peers:
        x_copy(own_slot, peer).start()
    sums = rows_out[...]
    for peer in reversed(peers):
        x_copy(peer, peer).wait_recv()
        sums = sums + rows_in[peer]
    rows_out_sum = sums
    inverse = lax.rsqrt(rows_out_sum[:, 0:1] / width + EPSILON)
    coef = inverse * inverse * inverse * rows_out_sum[:, 1:2] / width
    for b in range(2):
        at_role = jnp.where(core == b, 0, 1)
        inv_ref[at_role] = jnp.broadcast_to(inverse[b], (HD, tokens)).T
        coef_ref[at_role] = jnp.broadcast_to(coef[b], (HD, tokens)).T

    for role in range(2):
        for j in range(half):
            at = lanes(j)
            ga = inv_ref[role] * scaled_ref[role, :, at] - coef_ref[role] * att_ref[role, :, at]
            ga = ga.astype(bf16)
            ga_ref[role, :, at] = ga
            bpair[block[role], j] = dot(qt_ref[role, j], ga, NN)

    from_first, from_second = flag(sg_ref[c0] < c0), flag(sg_ref[c1] < c0)
    for j in range(half):
        put(bsum_out, j, from_first * bpair[0, j] + from_second * bpair[1, j])
    bsum_in[chip] = bsum_out[chip]
    chip_start(2, bsum_out, bsum_in)

    def local_backward(role, to_normed, to_gq, to_gk, to_gv, first):
        def one(j, _):
            at = lanes(j)
            to = lanes(first + j)
            ga = ga_ref[role, :, at]
            normed = att_ref[role, :, at] * inv_ref[role] * gain_ref[:, lanes(mine + j)]
            to_normed[:, to] = normed.astype(bf16)
            scores = dot(ga, v_ref[role, :, at], NT)
            scores = jnp.where(same_ref[role] > 0.5, scores, 0.0).astype(bf16)
            part = dot(ga * first_ref[role], carry_ref[role, j], NT)
            to_gq[:, to] = (dot(scores, k_ref[role, :, at], NN) + part).astype(bf16)
            to_gk[:, to] = dot(scores, q_ref[role, :, at], TN)
            to_gv[:, to] = dot(weights_ref[role, j], ga, TN)
            return _

        lax.fori_loop(0, half, one, 0)

    local_backward(1, normed_out, gq_out, gk_out, gv_out, 0)
    for copy in outs:
        copy.start()

    chip_wait(2, bsum_out, bsum_in)
    inner = [[None] * ring for _ in range(lines)]
    for i in range(ring - 1, -1, -1):
        for line in range(lines):
            w = line * ring + i
            if i == ring - 1:
                inner[line][i] = jnp.zeros((piece, HD), f32)
            else:
                value = bsum_in[w + 1].astype(f32)
                if i < ring - 2:
                    value = value + flag(sg_ref[2 * w + 4] <= 2 * w + 1) * inner[line][i + 1]
                inner[line][i] = flag(sg_ref[2 * w + 2] <= 2 * w + 1) * value
    run = None
    for line in range(lines - 1, -1, -1):
        behind = (line + 1) * ring
        for i in range(ring - 1, -1, -1):
            w = line * ring + i
            value = inner[line][i]
            if line + 1 < lines:
                value = value + flag(sg_ref[2 * behind] <= 2 * w + 1) * run
            brun_out[w] = value.astype(bf16)
        if line > 0:
            w = line * ring
            value = bsum_in[w].astype(f32) + flag(sg_ref[2 * w + 2] <= 2 * w - 1) * inner[line][0]
            if line + 1 < lines:
                value = value + flag(sg_ref[2 * behind] <= 2 * w - 1) * run
            run = value
    brun_in[chip] = brun_out[chip]
    chip_start(3, brun_out, brun_in)

    local_backward(0, normed_ref, gq_ref, gk_acc, gv_acc, mine)

    chip_wait(3, brun_out, brun_in)
    reach = flag(sg_ref[c2] <= c0)
    own_a, own_b = jnp.where(odd, 0.0, inside), jnp.where(odd, 1.0, reach)
    their_a, their_b = jnp.where(odd, inside, 0.0), jnp.where(odd, reach, 1.0)
    for j in range(half):
        bshare_out[j] = (their_a * bpair[1, j] + their_b * take(brun_in, j)).astype(bf16)
        close_copy(j, mine + j).start()
    for j in range(half):
        back_in[mine + j] = (own_a * bpair[1, j] + own_b * take(brun_in, j)).astype(bf16)

    for j in range(half):
        close_copy(j, theirs + j).wait_recv()

    for phase, src, dst in ((0, sum_out, sum_in), (1, run_out, run_in), (2, bsum_out, bsum_in), (3, brun_out, brun_in)):
        chip_sent(phase, src, dst)
    for copy in ins:
        copy.wait_send()
    for copy in outs:
        copy.wait_send()
        copy.wait_recv()
    for j in range(half):
        close_copy(j, mine + j).wait_send()
    for peer in peers:
        x_copy(own_slot, peer).wait_send()


def finish(
    normed_ref, gq_ref, gk_acc, gv_acc, kl_ref, vl_ref, back_ref,
    normed_out, gq_out, gk_out, gv_out,
    gk_ref, gv_ref, sem,
):
    heads = back_ref.shape[0]
    copies = [
        pltpu.make_async_copy(normed_ref, normed_out, sem.at[0]),
        pltpu.make_async_copy(gq_ref, gq_out, sem.at[1]),
    ]
    for copy in copies:
        copy.start()
    for h in range(heads):
        at = slice(h * HD, (h + 1) * HD)
        gk_ref[:, at] = (gk_acc[:, at] + dot(vl_ref[:, at], back_ref[h], NT)).astype(bf16)
        gv_ref[:, at] = (gv_acc[:, at] + dot(kl_ref[:, at], back_ref[h], NN)).astype(bf16)
        if h % 2 == 1:
            done = pl.ds((h - 1) * HD, 2 * HD)
            for i, (src, dst) in enumerate(((gk_ref, gk_out), (gv_ref, gv_out))):
                copy = pltpu.make_async_copy(src.at[:, done], dst.at[:, done], sem.at[h + 1 + i])
                copy.start()
                copies.append(copy)
    for copy in copies:
        copy.wait()


def solution(mesh):
    groups, spread = mesh.shape["seq"], mesh.shape["head"]
    chips = groups // 2
    ring = 4 if chips % 4 == 0 else 1

    def local(query_in, key_in, value_in, out_grad, norm_gain, doc_ids, start_group):
        tokens, columns = query_in.shape
        heads = columns // HD
        half = heads // 2
        vmem = pl.BlockSpec(memory_space=pltpu.VMEM)
        hbm = pl.BlockSpec(memory_space=pltpu.HBM)
        pair = pltpu.VMEM((2, half, HD, HD), f32)
        pieces = pltpu.VMEM((chips, half * HD // chips, HD), bf16)
        closed = pltpu.VMEM((half, HD, HD), bf16)
        narrow = pltpu.VMEM((2, tokens, HD), bf16)
        row = pltpu.VMEM((2, tokens, HD), f32)
        wide_b = pltpu.VMEM((tokens, columns), bf16)
        wide_f = pltpu.VMEM((tokens, columns), f32)
        half_b = pltpu.VMEM((tokens, columns // 2), bf16)
        half_f = pltpu.VMEM((tokens, columns // 2), f32)
        both_b = pltpu.VMEM((2, tokens, columns // 2), bf16)
        both_f = pltpu.VMEM((2, tokens, columns // 2), f32)
        dma = pltpu.SemaphoreType.DMA
        outs = pl.pallas_call(
            functools.partial(kernel, chips, ring, heads, spread, columns * spread),
            out_shape=[wide_b, wide_b, wide_f, wide_f, wide_b, wide_b, pltpu.VMEM((heads, HD, HD), bf16)],
            in_specs=[hbm] * 7,
            out_specs=[vmem] * 7,
            scratch_shapes=[
                pltpu.SMEM((groups,), jnp.int32),
                pltpu.VMEM((1, tokens), jnp.int32),
                pltpu.VMEM((1, columns), f32),
                *[both_b] * 4,
                pltpu.VMEM((1, tokens), jnp.int32),
                half_b,
                half_b,
                pltpu.VMEM((2, tokens, tokens), f32),
                narrow,
                pltpu.VMEM((tokens, HD), bf16),
                row,
                row,
                pltpu.VMEM((2, half, tokens, tokens), bf16),
                both_f,
                both_b,
                both_b,
                pltpu.VMEM((2, half, HD, tokens), bf16),
                both_f,
                *[pair, pieces, pieces, pieces, pieces],
                pltpu.VMEM((2, half, HD, HD), bf16),
                *[pair, pieces, pieces, pieces, pieces],
                closed,
                pltpu.VMEM((2, 2, tokens), f32),
                pltpu.VMEM((2 * spread, 2, 2, tokens), f32),
                half_b,
                half_b,
                half_f,
                half_f,
                dma((9,)),
                dma((4,)),
                dma((4,)),
                dma((5,)),
                dma((5,)),
                dma((4,)),
                dma((4,)),
                dma((half,)),
                dma((half,)),
                dma((2 * spread,)),
                dma((2 * spread,)),
                pltpu.SemaphoreType.REGULAR,
                pltpu.SemaphoreType.REGULAR,
            ],
            compiler_params=pltpu.CompilerParams(
                collective_id=0, has_side_effects=True, vmem_limit_bytes=62_300_000
            ),
            name="attention",
        )(
            start_group,
            doc_ids.reshape(1, tokens),
            query_in,
            key_in,
            value_in,
            out_grad,
            norm_gain.reshape(1, columns),
        )
        return pl.pallas_call(
            finish,
            out_shape=[jax.ShapeDtypeStruct((tokens, columns), bf16)] * 4,
            in_specs=[vmem] * 7,
            out_specs=[pl.BlockSpec(memory_space=pl.ANY)] * 4,
            scratch_shapes=[wide_b, wide_b, pltpu.SemaphoreType.DMA((heads + 2,))],
            compiler_params=pltpu.CompilerParams(vmem_limit_bytes=4 << 20),
            name="finish",
        )(*outs)

    wide = P("seq", "head")
    return jax.shard_map(
        local,
        mesh=mesh,
        in_specs=(wide, wide, wide, wide, P("head"), P("seq"), P()),
        out_specs=(wide, wide, wide, wide),
        check_vma=False,
    )
```

```python
import functools

import jax
import jax.numpy as jnp
from jax import lax
from jax.experimental import pallas as pl
from jax.experimental.pallas import tpu as pltpu
from jax.sharding import PartitionSpec as P

HD = 128
EPSILON = 1e-06
MESH = pl.DeviceIdType.MESH
f32, bf16 = jnp.float32, jnp.bfloat16


def dot(a, b, contract):
    return lax.dot_general(a, b, (contract, ((), ())), preferred_element_type=f32)


NN = ((1,), (0,))
NT = ((1,), (1,))
TN = ((0,), (0,))


def kernel(
    chips, ring, heads, spread, width,
    sg_hbm, doc_hbm, q_hbm, k_hbm, v_hbm, g_hbm, gain_hbm,
    normed_ref, gq_ref, gk_acc, gv_acc, kl_ref, vl_ref, back_in,
    sg_ref, doc_ref, gain_ref, q_ref, k_ref, v_ref, g_ref, doc_in, kx_ref, vx_ref,
    same_ref, first_ref, last_ref, inv_ref, coef_ref,
    weights_ref, att_ref, ga_ref, qf_ref, qt_ref, scaled_ref,
    pair, sum_out, sum_in, run_out, run_in, carry_ref,
    bpair, bsum_out, bsum_in, brun_out, brun_in, bshare_out,
    rows_out, rows_in, normed_out, gq_out, gk_out, gv_out,
    load_sem, chip_send, chip_recv, in_send, in_recv, out_send, out_recv, core_send, core_recv,
    x_send, x_recv, here, go,
):
    seq, col = lax.axis_index("seq"), lax.axis_index("head")
    chip, core = lax.div(seq, 2), lax.rem(seq, 2)
    partner = seq + 1 - 2 * core
    tokens = q_ref.shape[1]
    half = heads // 2
    piece = sum_out.shape[1]
    pieces = HD // piece
    mine, theirs = core * half, (1 - core) * half
    c0, c1, groups = 2 * chip, 2 * chip + 1, 2 * chips
    c2 = jnp.minimum(c0 + 2, groups - 1)
    lines = chips // ring
    block = (core, 1 - core)

    def columns(first):
        return pl.ds(pl.multiple_of(first * HD, HD), half * HD)

    loads = [
        pltpu.make_async_copy(src.at[:, columns(first)], dst, load_sem.at[i])
        for i, (src, first, dst) in enumerate(
            (
                (k_hbm, mine, k_ref.at[0]),
                (v_hbm, mine, v_ref.at[0]),
                (q_hbm, mine, q_ref.at[0]),
                (g_hbm, mine, g_ref.at[0]),
                (k_hbm, theirs, kx_ref),
                (v_hbm, theirs, vx_ref),
            )
        )
    ]
    smalls = [
        pltpu.make_async_copy(src, dst, load_sem.at[len(loads) + i])
        for i, (src, dst) in enumerate(((doc_hbm, doc_ref), (sg_hbm, sg_ref), (gain_hbm, gain_ref)))
    ]

    def hops(offset, size):
        return min(offset, size - offset)

    offsets = sorted(
        ((dz, dy) for dz in range(lines) for dy in range(ring) if dz or dy),
        key=lambda o: (-(hops(o[0], lines) + hops(o[1], ring)), -hops(o[1], ring), o),
    )
    chip_z, chip_y = lax.div(chip, ring), lax.rem(chip, ring)
    turn = 1 - 2 * core
    at_z = [lax.rem(chip_z + lines + turn * dz, lines) * ring for dz in range(lines)]
    at_y = [lax.rem(chip_y + ring + turn * dy, ring) for dy in range(ring)]
    others = [at_z[dz] + at_y[dy] for dz, dy in offsets]

    barrier = pltpu.get_barrier_semaphore()

    @pl.when(core == 0)
    def _():
        pl.semaphore_signal(barrier, inc=1, device_id=(partner, col), device_id_type=MESH)

    for other in others:
        pl.semaphore_signal(barrier, inc=1, device_id=(2 * other, col), device_id_type=MESH)
    for d in range(1, spread):
        pl.semaphore_signal(barrier, inc=1, device_id=(c0, lax.rem(col + d, spread)), device_id_type=MESH)

    for copy in smalls[:2] + loads[:2] + smalls[2:]:
        copy.start()

    def lanes(h):
        return pl.ds(pl.multiple_of(h * HD, HD), HD)

    def flag(condition):
        return jnp.where(condition, 1.0, 0.0).astype(f32)

    def to_partner(src, dst, send, recv):
        return pltpu.make_async_remote_copy(
            src_ref=src, dst_ref=dst, send_sem=send, recv_sem=recv, device_id=(partner, col), device_id_type=MESH
        )

    ins = [
        to_partner(src, dst, in_send.at[i], in_recv.at[i])
        for i, (src, dst) in enumerate(
            (
                (doc_hbm, doc_in),
                (k_hbm.at[:, columns(theirs)], k_ref.at[1]),
                (v_hbm.at[:, columns(theirs)], v_ref.at[1]),
                (q_hbm.at[:, columns(theirs)], q_ref.at[1]),
                (g_hbm.at[:, columns(theirs)], g_ref.at[1]),
            )
        )
    ]
    outs = [
        to_partner(src, dst.at[:, columns(mine)], out_send.at[i], out_recv.at[i])
        for i, (src, dst) in enumerate(
            ((normed_out, normed_ref), (gq_out, gq_ref), (gk_out, gk_acc), (gv_out, gv_acc))
        )
    ]

    def close_copy(j, slot):
        return to_partner(bshare_out.at[j], back_in.at[slot], core_send.at[j], core_recv.at[j])

    def chip_copy(phase, src, dst, at_src, at_dst, other):
        return pltpu.make_async_remote_copy(
            src_ref=src.at[at_src],
            dst_ref=dst.at[at_dst],
            send_sem=chip_send.at[phase],
            recv_sem=chip_recv.at[phase],
            device_id=(2 * other + core, col),
            device_id_type=MESH,
        )

    def chip_start(phase, src, dst):
        for other in others:
            chip_copy(phase, src, dst, other, chip, other).start()

    every = pl.ds(0, chips - 1)

    def chip_wait(phase, src, dst):
        chip_copy(phase, src, dst, every, every, others[0]).wait_recv()

    def chip_sent(phase, src, dst):
        chip_copy(phase, src, dst, every, every, others[0]).wait_send()

    def put(ref, j, state):
        ref[pl.ds(j * pieces, pieces)] = state.astype(bf16).reshape(pieces, piece, HD)

    def take(ref, j):
        return ref[pl.ds(j * pieces, pieces)].reshape(HD, HD).astype(f32)

    @pl.when(core == 1)
    def _():
        pl.semaphore_wait(barrier, 1)
        pl.semaphore_signal(here, inc=1, device_id=(partner, col), device_id_type=MESH)

    @pl.when(core == 0)
    def _():
        pl.semaphore_wait(here, 1)

    for copy in ins:
        copy.start()
    for load in loads[2:]:
        load.start()

    def edges(ids):
        docs = ids.astype(f32)
        return (
            docs,
            jnp.where(docs == docs[:, :1], 1.0, 0.0).astype(bf16),
            jnp.where(docs == docs[:, tokens - 1 :], 1.0, 0.0).astype(bf16),
        )

    def tails(role, last_row):
        for j in range(half):
            at = lanes(j)
            pair[block[role], j] = dot(k_ref[role, :, at].T * last_row, v_ref[role, :, at], NN)

    smalls[0].wait()
    marks = [edges(doc_ref[...]), None]
    loads[0].wait()
    loads[1].wait()
    tails(0, marks[0][2])
    for copy in ins[:3]:
        copy.wait_recv()
    marks[1] = edges(doc_in[...])
    tails(1, marks[1][2])

    smalls[1].wait()
    both = flag(sg_ref[c2] <= c0)
    for j in range(half):
        put(sum_out, j, pair[1, j] + both * pair[0, j])
    sum_in[chip] = sum_out[chip]

    @pl.when(core == 0)
    def _():
        pl.semaphore_wait(barrier, 2 * (chips - 1) + 2 * (spread - 1))
        pl.semaphore_signal(go, inc=1, device_id=(partner, col), device_id_type=MESH)

    @pl.when(core == 1)
    def _():
        pl.semaphore_wait(go, 1)

    chip_start(0, sum_out, sum_in)

    causal = lax.broadcasted_iota(jnp.int32, (tokens, tokens), 0) >= lax.broadcasted_iota(
        jnp.int32, (tokens, tokens), 1
    )
    for role in range(2):
        doc_row = jnp.broadcast_to(marks[role][0], (tokens, tokens))
        doc_col = doc_row.T
        same_ref[role] = jnp.where(causal & (doc_row == doc_col), 1.0, 0.0)
        own = doc_col[:, :HD]
        first_ref[role] = jnp.where(own == own[:1], 1.0, 0.0).astype(bf16)
        if role == 0:
            last_ref[...] = jnp.where(own == own[tokens - 1 :], 1.0, 0.0).astype(bf16)
    smalls[2].wait()
    for load in loads[2:]:
        load.wait()
    for copy in ins[3:]:
        copy.wait_recv()

    for role in range(2):

        def local_forward(j, _, role=role):
            at = lanes(j)
            query = q_ref[role, :, at]
            scores = dot(query, k_ref[role, :, at], NT)
            weights = jnp.where(same_ref[role] > 0.5, scores, 0.0).astype(bf16)
            weights_ref[role, j] = weights
            att_ref[role, :, at] = dot(weights, v_ref[role, :, at], NN)
            qf_ref[role, :, at] = query * first_ref[role]
            qt_ref[role, j] = query.T * marks[role][1]
            scaled_ref[role, :, at] = gain_ref[:, lanes(mine + j)] * g_ref[role, :, at].astype(f32)
            if role == 0:
                kl_ref[:, lanes(mine + j)] = k_ref[0, :, at] * last_ref[...]
                vl_ref[:, lanes(mine + j)] = v_ref[0, :, at] * last_ref[...]
                kl_ref[:, lanes(theirs + j)] = kx_ref[:, at] * last_ref[...]
                vl_ref[:, lanes(theirs + j)] = vx_ref[:, at] * last_ref[...]
            return _

        lax.fori_loop(0, half, local_forward, 0)

    joins = [flag(sg_ref[2 * w] <= 2 * w - 1) for w in range(1, chips)]
    keeps = [flag(sg_ref[2 * w] < 2 * w - 2) for w in range(1, chips)]
    enters = [flag(sg_ref[2 * w] < 2 * (w // ring) * ring) for w in range(chips)]
    chip_wait(0, sum_out, sum_in)
    inner = [[jnp.zeros((piece, HD), f32)] for _ in range(lines)]
    for i in range(1, ring + 1):
        for line in range(lines):
            w = line * ring + i
            if w < chips:
                value = sum_in[w - 1].astype(f32)
                if i > 1:
                    value = value + keeps[w - 1] * inner[line][-1]
                inner[line].append(joins[w - 1] * value)
    run = None
    for line in range(lines):
        for i in range(ring):
            w = line * ring + i
            value = inner[line][i]
            if line > 0:
                value = value + enters[w] * run
            run_out[w] = value.astype(bf16)
        if line + 1 < lines:
            value = inner[line][ring]
            if line > 0:
                value = value + flag(sg_ref[2 * (line + 1) * ring] < 2 * line * ring) * run
            run = value
    run_in[chip] = run_out[chip]
    chip_start(1, run_out, run_in)
    chip_wait(1, run_out, run_in)

    odd = core == 1
    inside, through = flag(sg_ref[c1] <= c0), flag(sg_ref[c1] < c0)
    own_a, own_b = jnp.where(odd, inside, 0.0), jnp.where(odd, through, 1.0)
    their_a, their_b = jnp.where(odd, 0.0, inside), jnp.where(odd, 1.0, through)
    for j in range(half):
        state, entering = pair[0, j], take(run_in, j)
        carry_ref[0, j] = (own_a * state + own_b * entering).astype(bf16)
        carry_ref[1, j] = (their_a * state + their_b * entering).astype(bf16)

    ones = jnp.ones((16, HD), bf16)

    def across(x):
        high = x.astype(bf16)
        low = (x - high.astype(f32)).astype(bf16)
        return (dot(ones, high, NT) + dot(ones, low, NT))[0:1]

    for role in range(2):
        square = jnp.zeros((tokens, HD), f32)
        cross = jnp.zeros((tokens, HD), f32)
        for j in range(half):
            at = lanes(j)
            att = att_ref[role, :, at] + dot(qf_ref[role, :, at], carry_ref[role, j], NN)
            att_ref[role, :, at] = att
            square = square + att * att
            cross = cross + scaled_ref[role, :, at] * att
        rows_out[block[role], 0:1] = across(square)
        rows_out[block[role], 1:2] = across(cross)

    own_slot = 2 * col + core

    def x_copy(slot, peer):
        return pltpu.make_async_remote_copy(
            src_ref=rows_out,
            dst_ref=rows_in.at[slot],
            send_sem=x_send.at[peer],
            recv_sem=x_recv.at[slot],
            device_id=(c0 + lax.rem(peer, 2), lax.div(peer, 2)),
            device_id_type=MESH,
        )

    peers = [
        2 * lax.rem(col + d, spread) + lax.rem(core + e, 2)
        for d in sorted(range(spread), key=lambda d: -hops(d, spread))
        for e in range(2)
        if d or e
    ]
    for peer in peers:
        x_copy(own_slot, peer).start()
    sums = rows_out[...]
    for peer in reversed(peers):
        x_copy(peer, peer).wait_recv()
        sums = sums + rows_in[peer]
    inverse = lax.rsqrt(sums[:, 0:1] / width + EPSILON)
    coef = inverse * inverse * inverse * sums[:, 1:2] / width
    first_role = flag(core == 0)
    scales = [
        first_role * part[role] + (1.0 - first_role) * part[1 - role] for role in range(2) for part in (inverse, coef)
    ]
    by_token = jnp.concatenate(scales + scales, axis=0).T
    for role in range(2):
        inv_ref[role] = jnp.broadcast_to(by_token[:, 2 * role : 2 * role + 1], (tokens, HD))
        coef_ref[role] = jnp.broadcast_to(by_token[:, 2 * role + 1 : 2 * role + 2], (tokens, HD))

    for role in range(2):
        for j in range(half):
            at = lanes(j)
            ga = inv_ref[role] * scaled_ref[role, :, at] - coef_ref[role] * att_ref[role, :, at]
            ga = ga.astype(bf16)
            ga_ref[role, :, at] = ga
            bpair[block[role], j] = dot(qt_ref[role, j], ga, NN)

    from_first, from_second = flag(sg_ref[c0] < c0), flag(sg_ref[c1] < c0)
    for j in range(half):
        put(bsum_out, j, from_first * bpair[0, j] + from_second * bpair[1, j])
    bsum_in[chip] = bsum_out[chip]
    chip_start(2, bsum_out, bsum_in)

    def local_backward(role, to_normed, to_gq, to_gk, to_gv, first):
        def one(j, _):
            at = lanes(j)
            to = lanes(first + j)
            ga = ga_ref[role, :, at]
            normed = att_ref[role, :, at] * inv_ref[role] * gain_ref[:, lanes(mine + j)]
            to_normed[:, to] = normed.astype(bf16)
            scores = dot(ga, v_ref[role, :, at], NT)
            scores = jnp.where(same_ref[role] > 0.5, scores, 0.0).astype(bf16)
            part = dot(ga * first_ref[role], carry_ref[role, j], NT)
            to_gq[:, to] = (dot(scores, k_ref[role, :, at], NN) + part).astype(bf16)
            to_gk[:, to] = dot(scores, q_ref[role, :, at], TN)
            to_gv[:, to] = dot(weights_ref[role, j], ga, TN)
            return _

        lax.fori_loop(0, half, one, 0)

    local_backward(1, normed_out, gq_out, gk_out, gv_out, 0)
    for copy in outs:
        copy.start()

    chip_wait(2, bsum_out, bsum_in)
    inner = [[None] * ring for _ in range(lines)]
    for i in range(ring - 1, -1, -1):
        for line in range(lines):
            w = line * ring + i
            if i == ring - 1:
                inner[line][i] = jnp.zeros((piece, HD), f32)
            else:
                value = bsum_in[w + 1].astype(f32)
                if i < ring - 2:
                    value = value + flag(sg_ref[2 * w + 4] <= 2 * w + 1) * inner[line][i + 1]
                inner[line][i] = flag(sg_ref[2 * w + 2] <= 2 * w + 1) * value
    run = None
    for line in range(lines - 1, -1, -1):
        behind = (line + 1) * ring
        for i in range(ring - 1, -1, -1):
            w = line * ring + i
            value = inner[line][i]
            if line + 1 < lines:
                value = value + flag(sg_ref[2 * behind] <= 2 * w + 1) * run
            brun_out[w] = value.astype(bf16)
        if line > 0:
            w = line * ring
            value = bsum_in[w].astype(f32) + flag(sg_ref[2 * w + 2] <= 2 * w - 1) * inner[line][0]
            if line + 1 < lines:
                value = value + flag(sg_ref[2 * behind] <= 2 * w - 1) * run
            run = value
    brun_in[chip] = brun_out[chip]
    chip_start(3, brun_out, brun_in)

    local_backward(0, normed_ref, gq_ref, gk_acc, gv_acc, mine)

    chip_wait(3, brun_out, brun_in)
    reach = flag(sg_ref[c2] <= c0)
    own_a, own_b = jnp.where(odd, 0.0, inside), jnp.where(odd, 1.0, reach)
    their_a, their_b = jnp.where(odd, inside, 0.0), jnp.where(odd, reach, 1.0)
    for j in range(half):
        bshare_out[j] = (their_a * bpair[1, j] + their_b * take(brun_in, j)).astype(bf16)
        close_copy(j, mine + j).start()
    for j in range(half):
        back_in[mine + j] = (own_a * bpair[1, j] + own_b * take(brun_in, j)).astype(bf16)

    for j in range(half):
        close_copy(j, theirs + j).wait_recv()

    for phase, src, dst in ((0, sum_out, sum_in), (1, run_out, run_in), (2, bsum_out, bsum_in), (3, brun_out, brun_in)):
        chip_sent(phase, src, dst)
    for copy in ins:
        copy.wait_send()
    for copy in outs:
        copy.wait_send()
        copy.wait_recv()
    for j in range(half):
        close_copy(j, mine + j).wait_send()
    for peer in peers:
        x_copy(own_slot, peer).wait_send()


def finish(
    normed_ref, gq_ref, gk_acc, gv_acc, kl_ref, vl_ref, back_ref,
    normed_out, gq_out, gk_out, gv_out,
    gk_ref, gv_ref, sem,
):
    heads = back_ref.shape[0]
    copies = [
        pltpu.make_async_copy(normed_ref, normed_out, sem.at[0]),
        pltpu.make_async_copy(gq_ref, gq_out, sem.at[1]),
    ]
    for copy in copies:
        copy.start()
    for h in range(heads):
        at = slice(h * HD, (h + 1) * HD)
        gk_ref[:, at] = (gk_acc[:, at] + dot(vl_ref[:, at], back_ref[h], NT)).astype(bf16)
        gv_ref[:, at] = (gv_acc[:, at] + dot(kl_ref[:, at], back_ref[h], NN)).astype(bf16)
        if h % 2 == 1:
            done = pl.ds((h - 1) * HD, 2 * HD)
            for i, (src, dst) in enumerate(((gk_ref, gk_out), (gv_ref, gv_out))):
                copy = pltpu.make_async_copy(src.at[:, done], dst.at[:, done], sem.at[h + 1 + i])
                copy.start()
                copies.append(copy)
    for copy in copies:
        copy.wait()


def solution(mesh):
    groups, spread = mesh.shape["seq"], mesh.shape["head"]
    chips = groups // 2
    ring = 4 if chips % 4 == 0 else 1

    def local(query_in, key_in, value_in, out_grad, norm_gain, doc_ids, start_group):
        tokens, columns = query_in.shape
        heads = columns // HD
        half = heads // 2
        vmem = pl.BlockSpec(memory_space=pltpu.VMEM)
        hbm = pl.BlockSpec(memory_space=pltpu.HBM)
        pair = pltpu.VMEM((2, half, HD, HD), f32)
        pieces = pltpu.VMEM((chips, half * HD // chips, HD), bf16)
        closed = pltpu.VMEM((half, HD, HD), bf16)
        narrow = pltpu.VMEM((2, tokens, HD), bf16)
        row = pltpu.VMEM((2, tokens, HD), f32)
        wide_b = pltpu.VMEM((tokens, columns), bf16)
        wide_f = pltpu.VMEM((tokens, columns), f32)
        half_b = pltpu.VMEM((tokens, columns // 2), bf16)
        half_f = pltpu.VMEM((tokens, columns // 2), f32)
        both_b = pltpu.VMEM((2, tokens, columns // 2), bf16)
        both_f = pltpu.VMEM((2, tokens, columns // 2), f32)
        dma = pltpu.SemaphoreType.DMA
        outs = pl.pallas_call(
            functools.partial(kernel, chips, ring, heads, spread, columns * spread),
            out_shape=[wide_b, wide_b, wide_f, wide_f, wide_b, wide_b, pltpu.VMEM((heads, HD, HD), bf16)],
            in_specs=[hbm] * 7,
            out_specs=[vmem] * 7,
            scratch_shapes=[
                pltpu.SMEM((groups,), jnp.int32),
                pltpu.VMEM((1, tokens), jnp.int32),
                pltpu.VMEM((1, columns), f32),
                *[both_b] * 4,
                pltpu.VMEM((1, tokens), jnp.int32),
                half_b,
                half_b,
                pltpu.VMEM((2, tokens, tokens), f32),
                narrow,
                pltpu.VMEM((tokens, HD), bf16),
                row,
                row,
                pltpu.VMEM((2, half, tokens, tokens), bf16),
                both_f,
                both_b,
                both_b,
                pltpu.VMEM((2, half, HD, tokens), bf16),
                both_f,
                *[pair, pieces, pieces, pieces, pieces],
                pltpu.VMEM((2, half, HD, HD), bf16),
                *[pair, pieces, pieces, pieces, pieces],
                closed,
                pltpu.VMEM((2, 2, tokens), f32),
                pltpu.VMEM((2 * spread, 2, 2, tokens), f32),
                half_b,
                half_b,
                half_f,
                half_f,
                dma((9,)),
                dma((4,)),
                dma((4,)),
                dma((5,)),
                dma((5,)),
                dma((4,)),
                dma((4,)),
                dma((half,)),
                dma((half,)),
                dma((2 * spread,)),
                dma((2 * spread,)),
                pltpu.SemaphoreType.REGULAR,
                pltpu.SemaphoreType.REGULAR,
            ],
            compiler_params=pltpu.CompilerParams(
                collective_id=0, has_side_effects=True, vmem_limit_bytes=62_300_000
            ),
            name="attention",
        )(
            start_group,
            doc_ids.reshape(1, tokens),
            query_in,
            key_in,
            value_in,
            out_grad,
            norm_gain.reshape(1, columns),
        )
        return pl.pallas_call(
            finish,
            out_shape=[jax.ShapeDtypeStruct((tokens, columns), bf16)] * 4,
            in_specs=[vmem] * 7,
            out_specs=[pl.BlockSpec(memory_space=pl.ANY)] * 4,
            scratch_shapes=[wide_b, wide_b, pltpu.SemaphoreType.DMA((heads + 2,))],
            compiler_params=pltpu.CompilerParams(vmem_limit_bytes=4 << 20),
            name="finish",
        )(*outs)

    wide = P("seq", "head")
    return jax.shard_map(
        local,
        mesh=mesh,
        in_specs=(wide, wide, wide, wide, P("head"), P("seq"), P()),
        out_specs=(wide, wide, wide, wide),
        check_vma=False,
    )
```
